256 devices in a mesh: term: 16 (over x, y), sector: 16 (over z, core).
Axes of the slice: x: 4, y: 4, z: 8, core: 2. Of those that a mesh axis runs over, the one named last changes fastest.
Arguments:
- wavefunction: float32 [16, 512, 512], P('sector'), may hold values from -120 to 120
- precond: float32 [16, 512, 512], P('sector', 'term'), may hold values from 0.05 to 4
- left_ops: float32 [16, 64, 512, 512], P('sector', 'term'), may hold values from -0.5 to 4.5
- right_ops: float32 [16, 64, 512, 512], P('sector', 'term'), may hold values from -1 to 2
- out_sector: int32 [16, 64], P('sector', 'term'), may hold values from 0 to 15, as said below
- live_counts: int32 [16, 16], P('sector', 'term'), may hold values from 1 to 4, as said below
Outputs:
- first_image: float32 [16, 512, 512], P('sector', 'term')
- correction: float32 [16, 512, 512], P('sector', 'term')
- second_image: float32 [16, 512, 512], P('sector', 'term')
The draws below stay inside these ranges and needn't reach their ends.
Inputs may be any that keep to these rules, and one draw needn't show every extreme that they name: Each term moves the charge by at most one sector: out_sector[s, j] differs from s by at most 1. `live_counts`: in every sector some device has all 4 slots live.
All inputs are finite; a program needn't handle non-finite values.
Results may differ from the reference program's by a relative error of at most 0.0003.
Values sent between devices are 32-bit elements; how exact they have to be, the bound alone decides.
No kernel may reach another device: no remote copies, remote signals or barrier semaphores. Data moves between devices by JAX's collectives and lax.ppermute only.
A program may use at most 64 MiB of HBM per device.

```python
import jax
import jax.numpy as jnp
from jax import lax

B = 512
CAP = 4
NSEC = 16
N_TERM = 16


def draw_wavefunction(key, part):
    key_values, key_rows, key_columns = jax.random.split(jax.random.fold_in(key, 11), 3)
    row_index = jnp.arange(B, dtype=jnp.float32)
    jitter = jax.random.uniform(key_rows, (B,), jnp.float32)
    row_scale = 10.0 ** ((row_index + jitter) / B)
    column_scale = 10.0 ** jax.random.uniform(key_columns, (B,), jnp.float32)
    sector_scale = 3.0 ** (jnp.arange(NSEC, dtype=jnp.float32) / max(NSEC - 1, 1))
    values = jax.random.truncated_normal(key_values, -4.0, 4.0, (NSEC, B, B), jnp.float32)
    return 0.1 * values * sector_scale[:, None, None] * row_scale[None, :, None] * column_scale[None, None, :]


def draw_out_sector(key, part):
    change = jax.random.randint(jax.random.fold_in(key, 23), (NSEC, N_TERM * CAP), -1, 2)
    sector_ids = jnp.arange(NSEC, dtype=jnp.int32)[:, None]
    target = sector_ids + change
    target = jnp.where(target < 0, sector_ids + 1, target)
    target = jnp.where(target > NSEC - 1, sector_ids - 1, target)
    return target.astype(jnp.int32)


def draw_live_counts(key, part):
    key_busy, key_pick = jax.random.split(jax.random.fold_in(key, 37), 2)
    busy = jax.random.randint(key_busy, (NSEC, N_TERM), 0, 10) < 3
    counts = jnp.where(busy, CAP, 1)
    chosen = jax.random.randint(key_pick, (NSEC,), 0, N_TERM)
    columns = jnp.arange(N_TERM, dtype=jnp.int32)[None, :]
    counts = jnp.where(columns == chosen[:, None], CAP, counts)
    return counts.astype(jnp.int32)


def sector_strengths(key):
    key_order, key_jitter = jax.random.split(jax.random.fold_in(key, 53), 2)
    order = jax.random.permutation(key_order, NSEC).astype(jnp.float32)
    jitter = jax.random.uniform(key_jitter, (NSEC,), jnp.float32)
    return 4.0 ** ((order + jitter) / NSEC)


def diagonal_weights(key, part):
    targets = draw_out_sector(key, part)
    counts = draw_live_counts(key, part)
    slot_ids = jnp.arange(N_TERM * CAP, dtype=jnp.int32) % CAP
    alive = slot_ids[None, :] < jnp.repeat(counts, CAP, axis=1)
    sector_ids = jnp.arange(NSEC, dtype=jnp.int32)[:, None]
    on_diagonal = jnp.logical_and(alive, targets == sector_ids)
    how_many = jnp.sum(on_diagonal.astype(jnp.float32), axis=1)
    strength = sector_strengths(key)
    effective = jnp.where(how_many > 0.5, strength, 0.0)
    per_slot = jnp.where(on_diagonal, (strength / jnp.maximum(how_many, 1.0))[:, None], 0.0)
    return (per_slot.astype(jnp.float32), effective.astype(jnp.float32))


def draw_left_ops(key, part):
    per_slot, effective = diagonal_weights(key, part)
    noise = jax.random.truncated_normal(jax.random.fold_in(key, 61), -4.0, 4.0, (NSEC, N_TERM * CAP, B, B), jnp.float32)
    noise = noise / jnp.sqrt(jnp.float32(B * N_TERM * CAP))
    identity = jnp.eye(B, dtype=jnp.float32)
    return noise + per_slot[:, :, None, None] * identity[None, None, :, :]


def draw_right_ops(key, part):
    noise = jax.random.truncated_normal(jax.random.fold_in(key, 67), -4.0, 4.0, (NSEC, N_TERM * CAP, B, B), jnp.float32)
    noise = noise / jnp.sqrt(jnp.float32(B))
    identity = jnp.eye(B, dtype=jnp.float32)
    return noise + identity[None, None, :, :]


def draw_precond(key, part):
    per_slot, effective = diagonal_weights(key, part)
    spread = jax.random.uniform(jax.random.fold_in(key, 71), (NSEC, B, B), jnp.float32, 0.0, 1.0)
    entries = 0.25 * 8.0 ** spread
    return entries / (effective + 0.5)[:, None, None]


def setup_inputs(seed: int = 0) -> dict:
    arg_keys = jax.random.split(jax.random.key(seed), 7)
    return {
        "wavefunction": draw_wavefunction(jax.random.fold_in(arg_keys[6], 71), 0),
        "precond": draw_precond(jax.random.fold_in(arg_keys[6], 71), 0),
        "left_ops": draw_left_ops(jax.random.fold_in(arg_keys[6], 71), 0),
        "right_ops": draw_right_ops(jax.random.fold_in(arg_keys[6], 71), 0),
        "out_sector": draw_out_sector(jax.random.fold_in(arg_keys[6], 71), 0),
        "live_counts": draw_live_counts(jax.random.fold_in(arg_keys[6], 71), 0),
    }


def matmul(first_op, second_op):
    return jnp.dot(first_op, second_op, precision=lax.Precision.HIGHEST, preferred_element_type=jnp.float32)


def apply_hamiltonian(field, left_ops, right_ops, out_sector, alive):
    def sector_step(totals, inputs):
        center, left_stack, right_stack, destinations, flags = inputs

        def slot_step(running, slot_data):
            left_one, right_one, destination, alive_flag = slot_data
            product = matmul(matmul(left_one, center), right_one)
            return running.at[destination].add(product * alive_flag), None

        totals, _ = lax.scan(slot_step, totals, (left_stack, right_stack, destinations, flags))
        return totals, None

    totals, _ = lax.scan(sector_step, jnp.zeros_like(field), (field, left_ops, right_ops, out_sector, alive))
    return totals


def reference(wavefunction, precond, left_ops, right_ops, out_sector, live_counts):
    slot_ids = jnp.arange(N_TERM * CAP, dtype=jnp.int32) % CAP
    alive = (slot_ids[None, :] < jnp.repeat(live_counts, CAP, axis=1)).astype(jnp.float32)
    first_image = apply_hamiltonian(wavefunction, left_ops, right_ops, out_sector, alive)
    norm_sq = jnp.sum(wavefunction * wavefunction)
    rayleigh = jnp.sum(wavefunction * first_image) / norm_sq
    raw = precond * (first_image - rayleigh * wavefunction)
    correction = raw - (jnp.sum(wavefunction * raw) / norm_sq) * wavefunction
    second_image = apply_hamiltonian(correction, left_ops, right_ops, out_sector, alive)
    return first_image, correction, second_image
```

```python
import functools

import jax
import jax.numpy as jnp
from jax import lax
from jax.experimental import pallas as pl
from jax.experimental.pallas import tpu as pltpu
from jax.sharding import Mesh
from jax.sharding import PartitionSpec as P

TERM = ("term_0", "term_1")
SECTOR = ("sector_0", "sector_1")
TERM_SECTOR = ("term_0", "term_1", "sector_0", "sector_1")
CHUNKS = 2


def shifted(block, distance):
    count = lax.axis_size(SECTOR)
    route = [(i, i + distance) for i in range(count) if 0 <= i + distance < count]
    return lax.ppermute(block, SECTOR, route)


def halves(x):
    high = x.astype(jnp.bfloat16)
    low = (x - high.astype(jnp.float32)).astype(jnp.bfloat16)
    return high, low


def product(a_high, a_low, b_high, b_low):
    dot = functools.partial(jnp.dot, preferred_element_type=jnp.float32)
    return dot(a_high, b_high) + (dot(a_high, b_low) + dot(a_low, b_high))


def accumulate(slot, meta, left, right, field_high, field_low, outs):
    peers, rows, width = left.shape[1:]

    @pl.when(slot == 0)
    def _():
        for out in outs:
            out[...] = jnp.zeros_like(out)

    @pl.when(slot < meta[0])
    def _():
        left_high, left_low = halves(left[0].reshape(peers * rows, width))
        inner = product(left_high, left_low, field_high[...], field_low[...])
        inner_high, inner_low = halves(inner)
        right_high, right_low = halves(right[0])
        result = product(inner_high, inner_low, right_high, right_low)
        result = result.reshape(peers, rows, width)
        for side in range(3):

            @pl.when(meta[1 + slot] == side)
            def _(out=outs[side]):
                out[...] += result


def first_kernel(meta, left, right, field, low_out, mid_out, high_out, field_high, field_low):
    slot = pl.program_id(0)

    @pl.when(slot == 0)
    def _():
        field_high[...], field_low[...] = halves(field[...])

    accumulate(slot, meta, left, right, field_high, field_low, (low_out, mid_out, high_out))


def second_kernel(meta, coefs, left, right, field, scaling, *rest):
    images = rest[:CHUNKS]
    low_out, mid_out, high_out, field_high, field_low = rest[CHUNKS:]
    slot = pl.program_id(0)

    @pl.when(slot == 0)
    def _():
        for c in range(CHUNKS):
            peers, rows, width = images[c].shape
            base = pl.ds(c * rows, rows)
            vector = field[:, base]
            raw = scaling[:, base] * (images[c][...] - coefs[0] * vector)
            correction = raw - coefs[1] * vector
            field_high[:, base], field_low[:, base] = halves(correction)

    peers, slab, width = field.shape
    accumulate(
        slot,
        meta,
        left,
        right,
        field_high.reshape(peers * slab, width),
        field_low.reshape(peers * slab, width),
        (low_out, mid_out, high_out),
    )


def image_chunk(chunk, meta, left_stack, right_stack, field, extra=None):
    slots, width, _ = right_stack.shape
    peers = left_stack.shape[1]
    slab = left_stack.shape[2]
    rows = slab // CHUNKS

    def live(slot, meta, *_):
        return jnp.minimum(slot, meta[0] - 1)

    left_spec = pl.BlockSpec(
        (1, peers, rows, width), lambda i, m, *r: (live(i, m), 0, chunk, 0)
    )
    right_spec = pl.BlockSpec((1, width, width), lambda i, m, *r: (live(i, m), 0, 0))

    def whole(shape):
        return pl.BlockSpec(shape, lambda i, m, *r: (0,) * len(shape))

    out_shape = (peers, rows, width)
    if extra is None:
        body, scalars, fields = first_kernel, (meta,), (field,)
        scratch_shape = (width, width)
    else:
        coefs, scaling, images = extra
        body, scalars, fields = second_kernel, (meta, coefs), (field, scaling, *images)
        scratch_shape = (peers, slab, width)
    return pl.pallas_call(
        body,
        out_shape=[jax.ShapeDtypeStruct(out_shape, jnp.float32)] * 3,
        grid_spec=pltpu.PrefetchScalarGridSpec(
            num_scalar_prefetch=len(scalars),
            grid=(slots,),
            in_specs=[left_spec, right_spec, *[whole(x.shape) for x in fields]],
            out_specs=[whole(out_shape)] * 3,
            scratch_shapes=[pltpu.VMEM(scratch_shape, jnp.bfloat16)] * 2,
        ),
        compiler_params=pltpu.CompilerParams(
            dimension_semantics=("arbitrary",), vmem_limit_bytes=32 << 20
        ),
        cost_estimate=pl.CostEstimate(
            flops=slots * 9 * width * width * width // CHUNKS,
            bytes_accessed=slots * 6 * width * width,
            transcendentals=0,
        ),
    )(*scalars, left_stack, right_stack, *fields)


def summed(blocks):
    low, mid, high = blocks
    total = mid + shifted(high, 1) + shifted(low, -1)
    return lax.all_to_all(total, TERM, 0, 0, tiled=True).sum(axis=0)


def copied(x):
    peers = lax.axis_size(TERM)
    return lax.all_to_all(jnp.broadcast_to(x[None], (peers, *x.shape)), TERM, 0, 0, tiled=True)


def per_device(wavefunction, precond, left_ops, right_ops, out_sector, live_counts):
    peers = lax.axis_size(TERM)
    width = wavefunction.shape[1]
    slots = left_ops.shape[1]
    slab = width // peers
    field = wavefunction[0]
    blocked = field.reshape(peers, slab, width)
    left_stack = left_ops[0].reshape(slots, peers, slab, width)
    right_stack = right_ops[0]
    scaling = precond[0]
    meta = jnp.concatenate([live_counts[0], out_sector[0] - lax.axis_index(SECTOR) + 1])

    full_scaling = copied(scaling)
    image_blocks = [image_chunk(c, meta, left_stack, right_stack, field) for c in range(CHUNKS)]
    images = [summed(b) for b in image_blocks]
    first_image = jnp.concatenate(images, axis=0)
    full_images = [copied(x) for x in images]
    own = lax.dynamic_index_in_dim(blocked, lax.axis_index(TERM), 0, keepdims=False)
    scaled = own * scaling
    sums = (
        jnp.sum(own * first_image),
        jnp.sum(own * own),
        jnp.sum(scaled * first_image),
        jnp.sum(scaled * own),
    )
    cross, norm_sq, scaled_cross, scaled_norm = lax.psum(sums, TERM_SECTOR)
    rayleigh = cross / norm_sq
    share = (scaled_cross - rayleigh * scaled_norm) / norm_sq
    correction = scaling * (first_image - rayleigh * own) - share * own
    coefs = jnp.stack([rayleigh, share])
    second_blocks = [
        image_chunk(
            c, meta, left_stack, right_stack, blocked, (coefs, full_scaling, full_images)
        )
        for c in range(CHUNKS)
    ]
    second_image = jnp.concatenate([summed(b) for b in second_blocks], axis=0)
    return (first_image[None], correction[None], second_image[None])


def solution(mesh):
    torus = Mesh(mesh.devices.reshape(4, 4, 8, 2), ("term_0", "term_1", "sector_0", "sector_1"))
    placed = (
        P(SECTOR, None, None),
        P(SECTOR, TERM, None),
        P(SECTOR, TERM, None, None),
        P(SECTOR, TERM, None, None),
        P(SECTOR, TERM),
        P(SECTOR, TERM),
    )
    return jax.shard_map(
        per_device,
        mesh=torus,
        in_specs=placed,
        out_specs=(P(SECTOR, TERM, None), P(SECTOR, TERM, None), P(SECTOR, TERM, None)),
        check_vma=False,
    )
```

```python
import functools

import jax
import jax.numpy as jnp
from jax import lax
from jax.experimental import pallas as pl
from jax.experimental.pallas import tpu as pltpu
from jax.sharding import Mesh
from jax.sharding import PartitionSpec as P

TERM = ("term_0", "term_1")
SECTOR = ("sector_0", "sector_1")
LANES = 128
EXTRA = 8
MIB = 1 << 20
F32 = jnp.float32


def shifted(block, distance):
    count = lax.axis_size(SECTOR)
    route = [(i, i + distance) for i in range(count) if 0 <= i + distance < count]
    return lax.ppermute(block, SECTOR, route)


def swapped(x):
    return lax.all_to_all(x, TERM, 0, 0, tiled=True)


def over_sectors(x):
    for axis in SECTOR[::-1]:
        count = lax.axis_size(axis)
        mask = 1
        while mask < count:
            x = x + lax.ppermute(x, axis, [(i, i ^ mask) for i in range(count)])
            mask *= 2
    return x


def halves(x):
    high = x.astype(jnp.bfloat16)
    low = (x - high.astype(F32)).astype(jnp.bfloat16)
    return high, low


def product(a_high, a_low, b_high, b_low):
    dot = functools.partial(jnp.dot, preferred_element_type=F32)
    return dot(a_high, b_high) + (dot(a_high, b_low) + dot(a_low, b_high))


def accumulate(sector, count, target, left, right, field_high, field_low, outs):
    slot = pl.program_id(0)

    @pl.when(slot == 0)
    def _():
        for out in outs:
            out[...] = jnp.zeros_like(out)

    @pl.when(slot < count[0, 0])
    def _():
        left_high, left_low = halves(left[0])
        inner = product(left_high, left_low, field_high[...], field_low[...])
        inner_high, inner_low = halves(inner)
        right_high, right_low = halves(right[0])
        result = product(inner_high, inner_low, right_high, right_low)
        for side, out in enumerate(outs):

            @pl.when(target[0, slot] - sector == side - 1)
            def _(out=out):
                out[...] += result


def first_kernel(count, target, left, right, field, low_out, mid_out, high_out, f_high, f_low):
    @pl.when(pl.program_id(0) == 0)
    def _():
        f_high[...], f_low[...] = halves(field[...])

    outs = (low_out, mid_out, high_out)
    accumulate(lax.axis_index(SECTOR), count, target, left, right, f_high, f_low, outs)


def coefficients(sums):
    cross, norm_sq = sums[0:1, 0:1], sums[1:2, 0:1]
    scaled_cross, scaled_norm = sums[2:3, 0:1], sums[3:4, 0:1]
    rayleigh = cross / norm_sq
    share = (scaled_cross - rayleigh * scaled_norm) / norm_sq
    return rayleigh, share


def second_kernel(
    count, target, left, right, sums, field, scaling, image, low_out, mid_out, high_out, f_high, f_low
):
    @pl.when(pl.program_id(0) == 0)
    def _():
        rayleigh, share = coefficients(sums[...])
        vector = field[...]
        correction = scaling[...] * (image[...] - rayleigh * vector) - share * vector
        f_high[...], f_low[...] = halves(correction)

    outs = (low_out, mid_out, high_out)
    accumulate(lax.axis_index(SECTOR), count, target, left, right, f_high, f_low, outs)


def partial_image(body, counts, targets, left_stack, right_stack, fields):
    slots, width, _ = right_stack.shape

    def operand(i, count, target):
        return (jnp.minimum(i, count[0, 0] - 1), 0, 0)

    def whole(shape):
        return pl.BlockSpec(shape, lambda i, *_: (0,) * len(shape))

    block = (width, width)
    return pl.pallas_call(
        body,
        out_shape=[jax.ShapeDtypeStruct(block, F32)] * 3,
        grid_spec=pltpu.PrefetchScalarGridSpec(
            num_scalar_prefetch=2,
            grid=(slots,),
            in_specs=[
                pl.BlockSpec((1, width, width), operand),
                pl.BlockSpec((1, width, width), operand),
                *[whole(x.shape) for x in fields],
            ],
            out_specs=[whole(block)] * 3,
            scratch_shapes=[pltpu.VMEM(block, jnp.bfloat16)] * 2,
        ),
        compiler_params=pltpu.CompilerParams(
            dimension_semantics=("arbitrary",), vmem_limit_bytes=48 * MIB
        ),
        cost_estimate=pl.CostEstimate(
            flops=slots * 12 * width**3, bytes_accessed=slots * 8 * width**2, transcendentals=0
        ),
    )(counts, targets, left_stack, right_stack, *fields)


def tiles(x, slab, width):
    return [(c * slab, slice(c * LANES, (c + 1) * LANES)) for c in range(width // LANES)]


def combine_kernel(mid, upward, downward, field, scaling, packed, totals):
    peers, slab, width = mid.shape
    where = tiles(mid, slab, width)
    cross = jnp.zeros((slab, width), F32)
    scaled_cross = jnp.zeros((slab, width), F32)
    for peer in range(peers):
        total = mid[peer] + (upward[peer] + downward[peer])
        for row, lanes in where:
            packed[peer, row : row + slab] = total[:, lanes]
        weighted = field[peer] * total
        cross += weighted
        scaled_cross += scaling[peer] * weighted
    me = lax.axis_index(TERM)
    own = field[me]
    square = own * own
    parts = [cross, square, scaled_cross, scaling[me] * square]
    line = lax.broadcasted_iota(jnp.int32, (EXTRA, LANES), 0)
    tile = jnp.zeros((EXTRA, LANES), F32)
    for i, part in enumerate(parts):
        tile = jnp.where(line == i, jnp.sum(part, keepdims=True), tile)
    totals[...] = tile
    for peer in range(peers):
        packed[peer, len(where) * slab :] = totals[...]


def gathered_kernel(arrived, image, copies, sums):
    peers, slab, width = copies.shape
    total = arrived[0]
    for peer in range(1, peers):
        total += arrived[peer]
    where = tiles(image, slab, width)
    for row, lanes in where:
        image[:, lanes] = total[row : row + slab]
    for peer in range(peers):
        copies[peer] = image[...]
    sums[...] = total[len(where) * slab :]


def small_call(body, out_shapes, args, scratch=()):
    return pl.pallas_call(
        body,
        out_shape=[jax.ShapeDtypeStruct(s, F32) for s in out_shapes],
        scratch_shapes=scratch,
        compiler_params=pltpu.CompilerParams(vmem_limit_bytes=32 * MIB),
    )(*args)


def per_device(wavefunction, precond, left_ops, right_ops, out_sector, live_counts):
    peers = lax.axis_size(TERM)
    width = wavefunction.shape[1]
    slab = width // peers
    split = (peers, slab, width)
    packed_rows = slab * (width // LANES) + EXTRA
    field = wavefunction[0]
    scaling = precond[0]
    image_of = functools.partial(
        partial_image,
        counts=live_counts,
        targets=out_sector,
        left_stack=left_ops[0],
        right_stack=right_ops[0],
    )

    low, mid, high = image_of(first_kernel, fields=(field,))
    upward, downward = shifted(high, 1), shifted(low, -1)
    scaling_late, _ = lax.optimization_barrier((scaling, mid))
    full_scaling = swapped(jnp.broadcast_to(scaling_late[None], split))
    (packed,) = small_call(
        combine_kernel,
        [(peers, packed_rows, LANES)],
        [*[x.reshape(split) for x in (mid, upward, downward, field)], full_scaling],
        [pltpu.VMEM((EXTRA, LANES), F32)],
    )
    first_image, copies, sums = small_call(
        gathered_kernel, [(slab, width), split, (EXTRA, LANES)], [swapped(packed)]
    )
    full_image = swapped(copies)
    sums = over_sectors(sums)

    own = lax.dynamic_index_in_dim(
        field.reshape(split), lax.axis_index(TERM), 0, keepdims=False
    )
    rayleigh, share = coefficients(sums)
    correction = scaling * (first_image - rayleigh * own) - share * own

    fields = (sums, field, full_scaling.reshape(field.shape), full_image.reshape(field.shape))
    low, mid, high = image_of(second_kernel, fields=fields)
    total = mid + shifted(high, 1) + shifted(low, -1)
    second_image = swapped(total.reshape(split)).sum(axis=0)
    return (first_image[None], correction[None], second_image[None])


def solution(mesh):
    torus = Mesh(mesh.devices.reshape(4, 4, 8, 2), ("term_0", "term_1", "sector_0", "sector_1"))
    placed = (
        P(SECTOR, None, None),
        P(SECTOR, TERM, None),
        P(SECTOR, TERM, None, None),
        P(SECTOR, TERM, None, None),
        P(SECTOR, TERM),
        P(SECTOR, TERM),
    )
    return jax.shard_map(
        per_device,
        mesh=torus,
        in_specs=placed,
        out_specs=(P(SECTOR, TERM, None), P(SECTOR, TERM, None), P(SECTOR, TERM, None)),
        check_vma=False,
    )
```

```python
import functools

import jax
import jax.numpy as jnp
from jax import lax
from jax.experimental import pallas as pl
from jax.experimental.pallas import tpu as pltpu
from jax.sharding import Mesh
from jax.sharding import PartitionSpec as P

TERM = ("term_0", "term_1")
SECTOR = ("sector_0", "sector_1")
LANES = 128
EXTRA = 8
MIB = 1 << 20
KERNEL_VMEM = 20 * MIB
F32 = jnp.float32


def moved(crossing, local):
    count = lax.axis_size(SECTOR)
    upward = [(i, i + 1) for i in range(1, count - 1, 2)]
    downward = [(j, i) for i, j in upward]
    swap = [(i, i ^ 1) for i in range(count)]
    return lax.ppermute(crossing, SECTOR, upward + downward), lax.ppermute(local, SECTOR, swap)


def swapped(x):
    return lax.all_to_all(x, TERM, 0, 0, tiled=True)


def over_sectors(x):
    for axis in SECTOR[::-1]:
        count = lax.axis_size(axis)
        mask = 1
        while mask < count:
            x = x + lax.ppermute(x, axis, [(i, i ^ mask) for i in range(count)])
            mask *= 2
    return x


def halves(x):
    high = x.astype(jnp.bfloat16)
    low = (x - high.astype(F32)).astype(jnp.bfloat16)
    return high, low


def product(a_high, a_low, b_high, b_low):
    dot = functools.partial(jnp.dot, preferred_element_type=F32)
    return dot(a_high, b_high) + (dot(a_high, b_low) + dot(a_low, b_high))


def accumulate(sector, count, target, left, right, field_high, field_low, outs):
    slot = pl.program_id(0)

    @pl.when(slot == 0)
    def _():
        for out in outs:
            out[...] = jnp.zeros_like(out)

    @pl.when(slot < count[0, 0])
    def _():
        left_high, left_low = halves(left[0])
        inner = product(left_high, left_low, field_high[...], field_low[...])
        inner_high, inner_low = halves(inner)
        right_high, right_low = halves(right[0])
        result = product(inner_high, inner_low, right_high, right_low)
        goal = target[0, slot]
        kept = goal == sector
        swapped_here = goal == (sector ^ 1)
        roles = (jnp.logical_not(kept | swapped_here), kept, swapped_here)
        for role, out in zip(roles, outs):

            @pl.when(role)
            def _(out=out):
                out[...] += result


def first_kernel(count, target, left, right, field, crossing, kept, local, f_high, f_low):
    @pl.when(pl.program_id(0) == 0)
    def _():
        f_high[...], f_low[...] = halves(field[...])

    outs = (crossing, kept, local)
    accumulate(lax.axis_index(SECTOR), count, target, left, right, f_high, f_low, outs)


def coefficients(sums):
    cross, norm_sq = sums[0:1, 0:1], sums[1:2, 0:1]
    scaled_cross, scaled_norm = sums[2:3, 0:1], sums[3:4, 0:1]
    rayleigh = cross / norm_sq
    share = (scaled_cross - rayleigh * scaled_norm) / norm_sq
    return rayleigh, share


def second_kernel(
    count, target, left, right, sums, field, scaling, image, crossing, kept, local, f_high, f_low
):
    @pl.when(pl.program_id(0) == 0)
    def _():
        rayleigh, share = coefficients(sums[...])
        vector = field[...]
        correction = scaling[...] * (image[...] - rayleigh * vector) - share * vector
        f_high[...], f_low[...] = halves(correction)

    outs = (crossing, kept, local)
    accumulate(lax.axis_index(SECTOR), count, target, left, right, f_high, f_low, outs)


def partial_image(body, counts, targets, left_stack, right_stack, fields, streamed=False):
    slots, width, _ = right_stack.shape

    def operand(i, count):
        return (jnp.minimum(i, count[0, 0] - 1), 0, 0)

    in_vmem = pl.BlockSpec(memory_space=pltpu.VMEM)
    targets, left_stack, right_stack = (
        pltpu.with_memory_space_constraint(x, pltpu.HBM)
        for x in (targets, left_stack, right_stack)
    )
    block = (width, width)
    field_spec = in_vmem
    if streamed:
        fields = [pltpu.with_memory_space_constraint(x, pltpu.HBM) for x in fields]
        field_spec = pl.BlockSpec(block, lambda i, *_: (0, 0), pipeline_mode=pl.Buffered(1))
    return pl.pallas_call(
        body,
        out_shape=[jax.ShapeDtypeStruct(block, F32)] * 3,
        grid_spec=pltpu.PrefetchScalarGridSpec(
            num_scalar_prefetch=1,
            grid=(slots,),
            in_specs=[
                pl.BlockSpec(targets.shape, lambda i, *_: (0, 0), memory_space=pltpu.SMEM),
                pl.BlockSpec((1, width, width), operand),
                pl.BlockSpec((1, width, width), operand),
                *[field_spec] * len(fields),
            ],
            out_specs=[in_vmem] * 3,
            scratch_shapes=[pltpu.VMEM(block, jnp.bfloat16)] * 2,
        ),
        compiler_params=pltpu.CompilerParams(
            dimension_semantics=("arbitrary",), vmem_limit_bytes=KERNEL_VMEM
        ),
        cost_estimate=pl.CostEstimate(
            flops=slots * 12 * width**3, bytes_accessed=slots * 8 * width**2, transcendentals=0
        ),
    )(counts, targets, left_stack, right_stack, *fields)


def tiles(x, slab, width):
    return [(c * slab, slice(c * LANES, (c + 1) * LANES)) for c in range(width // LANES)]


def combine_kernel(mid, crossed, local, field, scaling, packed, totals):
    peers, slab, width = mid.shape
    where = tiles(mid, slab, width)
    cross = jnp.zeros((slab, width), F32)
    scaled_cross = jnp.zeros((slab, width), F32)
    for peer in range(peers):
        total = mid[peer] + (crossed[peer] + local[peer])
        for row, lanes in where:
            packed[peer, row : row + slab] = total[:, lanes]
        weighted = field[peer] * total
        cross += weighted
        scaled_cross += scaling[peer] * weighted
    me = lax.axis_index(TERM)
    own = field[me]
    square = own * own
    parts = [cross, square, scaled_cross, scaling[me] * square]
    line = lax.broadcasted_iota(jnp.int32, (EXTRA, LANES), 0)
    tile = jnp.zeros((EXTRA, LANES), F32)
    for i, part in enumerate(parts):
        tile = jnp.where(line == i, jnp.sum(part, keepdims=True), tile)
    totals[...] = tile
    for peer in range(peers):
        packed[peer, len(where) * slab :] = totals[...]


def gathered_kernel(arrived, image, copies, sums, sent):
    peers, slab, width = copies.shape
    total = arrived[0]
    for peer in range(1, peers):
        total += arrived[peer]
    where = tiles(image, slab, width)
    for row, lanes in where:
        image[:, lanes] = total[row : row + slab]
    fills = [pltpu.make_async_copy(image, copies.at[i], sent.at[i]) for i in range(peers)]
    for fill in fills:
        fill.start()
    sums[...] = total[len(where) * slab :]
    for fill in fills:
        fill.wait()


def small_call(body, out_shapes, args, scratch=(), spaces=None):
    spaces = spaces or [pltpu.VMEM] * len(out_shapes)
    return pl.pallas_call(
        body,
        in_specs=[pl.BlockSpec(memory_space=pltpu.VMEM)] * len(args),
        out_specs=[pl.BlockSpec(memory_space=space) for space in spaces],
        out_shape=[
            pltpu.HBM(s, F32) if space == pltpu.HBM else jax.ShapeDtypeStruct(s, F32)
            for s, space in zip(out_shapes, spaces)
        ],
        scratch_shapes=scratch,
        compiler_params=pltpu.CompilerParams(vmem_limit_bytes=32 * MIB),
    )(*args)


def per_device(wavefunction, precond, left_ops, right_ops, out_sector, live_counts):
    peers = lax.axis_size(TERM)
    width = wavefunction.shape[1]
    slab = width // peers
    split = (peers, slab, width)
    packed_rows = slab * (width // LANES) + EXTRA
    field = wavefunction[0]
    scaling = precond[0]
    image_of = functools.partial(
        partial_image,
        counts=live_counts,
        targets=out_sector,
        left_stack=left_ops[0],
        right_stack=right_ops[0],
    )

    crossing, mid, local = image_of(first_kernel, fields=(field,), streamed=True)
    crossed, local = moved(crossing, local)
    scaling_late, _ = lax.optimization_barrier((scaling, mid))
    full_scaling = swapped(jnp.broadcast_to(scaling_late[None], split))
    (packed,) = small_call(
        combine_kernel,
        [(peers, packed_rows, LANES)],
        [*[x.reshape(split) for x in (mid, crossed, local, field)], full_scaling],
        [pltpu.VMEM((EXTRA, LANES), F32)],
    )
    first_image, copies, sums = small_call(
        gathered_kernel, [(slab, width), split, (EXTRA, LANES)], [swapped(packed)],
        [pltpu.SemaphoreType.DMA((peers,))], [pltpu.VMEM, pltpu.HBM, pltpu.VMEM],
    )
    full_image = swapped(copies)
    sums = over_sectors(sums)

    own = lax.dynamic_index_in_dim(
        field.reshape(split), lax.axis_index(TERM), 0, keepdims=False
    )
    rayleigh, share = coefficients(sums)
    correction = scaling * (first_image - rayleigh * own) - share * own

    fields = (sums, field, full_scaling.reshape(field.shape), full_image.reshape(field.shape))
    crossing, mid, local = image_of(second_kernel, fields=fields)
    crossed, local = moved(crossing, local)
    total = mid + crossed + local
    second_image = swapped(total.reshape(split)).sum(axis=0)
    return (first_image[None], correction[None], second_image[None])


def solution(mesh):
    torus = Mesh(mesh.devices.reshape(4, 4, 8, 2), ("term_0", "term_1", "sector_0", "sector_1"))
    placed = (
        P(SECTOR, None, None),
        P(SECTOR, TERM, None),
        P(SECTOR, TERM, None, None),
        P(SECTOR, TERM, None, None),
        P(SECTOR, TERM),
        P(SECTOR, TERM),
    )
    return jax.shard_map(
        per_device,
        mesh=torus,
        in_specs=placed,
        out_specs=(P(SECTOR, TERM, None), P(SECTOR, TERM, None), P(SECTOR, TERM, None)),
        check_vma=False,
    )
```

```python
import functools

import jax
import jax.numpy as jnp
from jax import lax
from jax.experimental import pallas as pl
from jax.experimental.pallas import tpu as pltpu
from jax.sharding import Mesh
from jax.sharding import PartitionSpec as P

TERM = ("term_0", "term_1")
SECTOR = ("sector_0", "sector_1")
LANES = 128
EXTRA = 8
MIB = 1 << 20
KERNEL_VMEM = 20 * MIB
F32 = jnp.float32


def moved(crossing, local):
    count = lax.axis_size(SECTOR)
    upward = [(i, i + 1) for i in range(1, count - 1, 2)]
    downward = [(j, i) for i, j in upward]
    swap = [(i, i ^ 1) for i in range(count)]
    return lax.ppermute(crossing, SECTOR, upward + downward), lax.ppermute(local, SECTOR, swap)


def from_ring(x, axis):
    size = lax.axis_size(axis)
    steps = [[(i, (i + k) % size) for i in range(size)] for k in range(1, size)]
    return [x, *[lax.ppermute(x, axis, pairs) for pairs in steps]]


def swapped(x):
    return lax.all_to_all(x, TERM, 0, 0, tiled=True)


def sector_steps():
    for axis in SECTOR[::-1]:
        count = lax.axis_size(axis)
        mask = 1
        while mask < count:
            yield functools.partial(exchanged, axis=axis, mask=mask)
            mask *= 2


def exchanged(x, axis, mask):
    pairs = [(i, i ^ mask) for i in range(lax.axis_size(axis))]
    return x + lax.ppermute(x, axis, pairs)


def over_sectors(x, steps=slice(None)):
    for step in list(sector_steps())[steps]:
        x = step(x)
    return x


def halves(x):
    high = x.astype(jnp.bfloat16)
    low = (x - high.astype(F32)).astype(jnp.bfloat16)
    return high, low


def product(a_high, a_low, b_high, b_low):
    dot = functools.partial(jnp.dot, preferred_element_type=F32)
    return dot(a_high, b_high) + (dot(a_high, b_low) + dot(a_low, b_high))


def accumulate(sector, count, target, left, right, field_high, field_low, outs):
    slot = pl.program_id(0)

    @pl.when(slot == 0)
    def _():
        for out in outs:
            out[...] = jnp.zeros_like(out)

    @pl.when(slot < count[0, 0])
    def _():
        left_high, left_low = halves(left[0])
        inner = product(left_high, left_low, field_high[...], field_low[...])
        inner_high, inner_low = halves(inner)
        right_high, right_low = halves(right[0])
        result = product(inner_high, inner_low, right_high, right_low)
        goal = target[0, slot]
        kept = goal == sector
        swapped_here = goal == (sector ^ 1)
        roles = (jnp.logical_not(kept | swapped_here), kept, swapped_here)
        for role, out in zip(roles, outs):

            @pl.when(role)
            def _(out=out):
                out[...] += result


def first_kernel(count, target, left, right, field, crossing, kept, local, f_high, f_low):
    @pl.when(pl.program_id(0) == 0)
    def _():
        f_high[...], f_low[...] = halves(field[...])

    outs = (crossing, kept, local)
    accumulate(lax.axis_index(SECTOR), count, target, left, right, f_high, f_low, outs)


def second_kernel(
    count,
    target,
    left,
    right,
    sums,
    field,
    image,
    *rest,
):
    ring, (crossing, kept, local, overlap, f_high, f_low) = rest[:-6], rest[-6:]
    peers, slab, width = field.shape

    @pl.when(pl.program_id(0) == 0)
    def _():
        rayleigh = sums[0:1, 0:1] / sums[1:2, 0:1]
        along_0, along_1 = (lax.axis_index(axis) for axis in TERM)
        size = ring[0].shape[0]
        weighted = jnp.zeros((slab, width), F32)
        for j, scaling in enumerate(ring):
            for k in range(size):
                peer = lax.rem(along_0 + len(ring) - j, len(ring)) * size
                peer += lax.rem(along_1 + size - k, size)
                vector = field[peer]
                raw = scaling[k] * (image[peer] - rayleigh * vector)
                f_high[peer], f_low[peer] = halves(raw)
                weighted += vector * raw
        overlap[...] = jnp.broadcast_to(jnp.sum(weighted, keepdims=True), overlap.shape)

    outs = (crossing, kept, local)
    flat = (peers * slab, width)
    f_high, f_low = f_high.reshape(flat), f_low.reshape(flat)
    accumulate(lax.axis_index(SECTOR), count, target, left, right, f_high, f_low, outs)


def partial_image(body, counts, targets, left_stack, right_stack, fields, extra=(), scratch=None, streamed=False):
    slots, width, _ = right_stack.shape

    def operand(i, count):
        return (jnp.minimum(i, count[0, 0] - 1), 0, 0)

    in_vmem = pl.BlockSpec(memory_space=pltpu.VMEM)
    targets, left_stack, right_stack = (
        pltpu.with_memory_space_constraint(x, pltpu.HBM)
        for x in (targets, left_stack, right_stack)
    )
    block = (width, width)
    field_spec = in_vmem
    if streamed:
        fields = [pltpu.with_memory_space_constraint(x, pltpu.HBM) for x in fields]
        field_spec = pl.BlockSpec(block, lambda i, *_: (0, 0), pipeline_mode=pl.Buffered(1))
    return pl.pallas_call(
        body,
        out_shape=[jax.ShapeDtypeStruct(x, F32) for x in (*[block] * 3, *extra)],
        grid_spec=pltpu.PrefetchScalarGridSpec(
            num_scalar_prefetch=1,
            grid=(slots,),
            in_specs=[
                pl.BlockSpec(targets.shape, lambda i, *_: (0, 0), memory_space=pltpu.SMEM),
                pl.BlockSpec((1, width, width), operand),
                pl.BlockSpec((1, width, width), operand),
                *[field_spec] * len(fields),
            ],
            out_specs=[in_vmem] * (3 + len(extra)),
            scratch_shapes=[pltpu.VMEM(scratch or block, jnp.bfloat16)] * 2,
        ),
        compiler_params=pltpu.CompilerParams(
            dimension_semantics=("arbitrary",), vmem_limit_bytes=KERNEL_VMEM
        ),
        cost_estimate=pl.CostEstimate(
            flops=slots * 12 * width**3, bytes_accessed=slots * 8 * width**2, transcendentals=0
        ),
    )(counts, targets, left_stack, right_stack, *fields)


def tiles(x, slab, width):
    return [(c * slab, slice(c * LANES, (c + 1) * LANES)) for c in range(width // LANES)]


def combine_kernel(mid, crossed, local, field, packed, sums):
    peers, slab, width = mid.shape
    where = tiles(mid, slab, width)
    cross = jnp.zeros((slab, width), F32)
    for peer in range(peers):
        total = mid[peer] + (crossed[peer] + local[peer])
        for row, lanes in where:
            packed[peer, row : row + slab] = total[:, lanes]
        cross += field[peer] * total
    own = field[lax.axis_index(TERM)]
    line = lax.broadcasted_iota(jnp.int32, (EXTRA, LANES), 0)
    sums[...] = jnp.where(
        line == 0, jnp.sum(cross, keepdims=True), jnp.sum(own * own, keepdims=True)
    )
    for peer in range(peers):
        packed[peer, len(where) * slab :] = sums[...]


def gathered_kernel(arrived, image, copies, sums):
    peers, slab, width = copies.shape
    total = arrived[0]
    for peer in range(1, peers):
        total += arrived[peer]
    where = tiles(image, slab, width)
    for row, lanes in where:
        image[:, lanes] = total[row : row + slab]
    for peer in range(peers):
        copies[peer] = image[...]
    sums[...] = total[len(where) * slab :]


def small_call(body, out_shapes, args, scratch=(), spaces=None):
    spaces = spaces or [pltpu.VMEM] * len(out_shapes)
    return pl.pallas_call(
        body,
        in_specs=[pl.BlockSpec(memory_space=pltpu.VMEM)] * len(args),
        out_specs=[
            pl.BlockSpec() if space == pltpu.HBM else pl.BlockSpec(memory_space=space)
            for space in spaces
        ],
        out_shape=[
            pltpu.HBM(s, F32) if space == pltpu.HBM else jax.ShapeDtypeStruct(s, F32)
            for s, space in zip(out_shapes, spaces)
        ],
        scratch_shapes=scratch,
        compiler_params=pltpu.CompilerParams(vmem_limit_bytes=32 * MIB),
    )(*args)


def per_device(wavefunction, precond, left_ops, right_ops, out_sector, live_counts):
    peers = lax.axis_size(TERM)
    width = wavefunction.shape[1]
    slab = width // peers
    split = (peers, slab, width)
    packed_rows = slab * (width // LANES) + EXTRA
    field = wavefunction[0]
    scaling = precond[0]
    image_of = functools.partial(
        partial_image,
        counts=live_counts,
        targets=out_sector,
        left_stack=left_ops[0],
        right_stack=right_ops[0],
    )

    crossing, mid, local = image_of(first_kernel, fields=(field,), streamed=True)
    crossed, local = moved(crossing, local)
    scaling_late, _ = lax.optimization_barrier((scaling, mid))
    stacked = jnp.stack(from_ring(scaling_late, TERM[1]))
    crossed, stacked = lax.optimization_barrier((crossed, stacked))
    ring = from_ring(stacked, TERM[0])
    (packed,) = small_call(
        combine_kernel,
        [(peers, packed_rows, LANES)],
        [x.reshape(split) for x in (mid, crossed, local, field)],
        [pltpu.VMEM((EXTRA, LANES), F32)],
    )
    arrived, *ring = lax.optimization_barrier((swapped(packed), *ring))
    first_image, copies, sums = small_call(
        gathered_kernel,
        [(slab, width), split, (EXTRA, LANES)],
        [arrived],
        spaces=[pltpu.VMEM, pltpu.HBM, pltpu.VMEM],
    )
    full_image = swapped(copies)
    sums = over_sectors(sums)

    fields = (sums, field.reshape(split), full_image, *ring)
    crossing, mid, local, overlap = image_of(
        second_kernel, fields=fields, extra=[(EXTRA, LANES)], scratch=split
    )
    crossed, local = moved(crossing, local)
    overlap = over_sectors(overlap, slice(0, 2))
    crossed, overlap = lax.optimization_barrier((crossed, overlap))
    total = mid + crossed + local
    overlap = over_sectors(overlap, slice(2, None))
    arrived = swapped(total.reshape(split))

    norm_sq = sums[1:2, 0:1]
    rayleigh = sums[0:1, 0:1] / norm_sq
    share = overlap[0:1, 0:1] / norm_sq
    own = lax.dynamic_index_in_dim(
        field.reshape(split), lax.axis_index(TERM), 0, keepdims=False
    )
    correction = scaling * (first_image - rayleigh * own) - share * own
    second_image = arrived.sum(axis=0) - share * first_image
    return (first_image[None], correction[None], second_image[None])


def solution(mesh):
    torus = Mesh(mesh.devices.reshape(4, 4, 8, 2), ("term_0", "term_1", "sector_0", "sector_1"))
    placed = (
        P(SECTOR, None, None),
        P(SECTOR, TERM, None),
        P(SECTOR, TERM, None, None),
        P(SECTOR, TERM, None, None),
        P(SECTOR, TERM),
        P(SECTOR, TERM),
    )
    return jax.shard_map(
        per_device,
        mesh=torus,
        in_specs=placed,
        out_specs=(P(SECTOR, TERM, None), P(SECTOR, TERM, None), P(SECTOR, TERM, None)),
        check_vma=False,
    )
```

```python
import functools

import jax
import jax.numpy as jnp
from jax import lax
from jax.experimental import pallas as pl
from jax.experimental.pallas import tpu as pltpu
from jax.sharding import Mesh
from jax.sharding import PartitionSpec as P

TERM = ("term_0", "term_1")
SECTOR = ("sector_0", "sector_1")
LANES = 128
EXTRA = 8
MIB = 1 << 20
KERNEL_VMEM = 20 * MIB
F32 = jnp.float32


def moved(crossing, local):
    count = lax.axis_size(SECTOR)
    upward = [(i, i + 1) for i in range(1, count - 1, 2)]
    downward = [(j, i) for i, j in upward]
    swap = [(i, i ^ 1) for i in range(count)]
    return lax.ppermute(crossing, SECTOR, upward + downward), lax.ppermute(local, SECTOR, swap)


def swapped(x):
    return lax.all_to_all(x, TERM, 0, 0, tiled=True)


def sector_steps():
    for axis in SECTOR[::-1]:
        count = lax.axis_size(axis)
        mask = 1
        while mask < count:
            yield functools.partial(exchanged, axis=axis, mask=mask)
            mask *= 2


def exchanged(x, axis, mask):
    pairs = [(i, i ^ mask) for i in range(lax.axis_size(axis))]
    return x + lax.ppermute(x, axis, pairs)


def over_sectors(x, steps=slice(None)):
    for step in list(sector_steps())[steps]:
        x = step(x)
    return x


def halves(x):
    high = x.astype(jnp.bfloat16)
    low = (x - high.astype(F32)).astype(jnp.bfloat16)
    return high, low


def product(a_high, a_low, b_high, b_low):
    dot = functools.partial(jnp.dot, preferred_element_type=F32)
    return dot(a_high, b_high) + (dot(a_high, b_low) + dot(a_low, b_high))


def accumulate(sector, count, target, left, right, field_high, field_low, outs):
    slot = pl.program_id(0)

    @pl.when(slot == 0)
    def _():
        for out in outs:
            out[...] = jnp.zeros_like(out)

    @pl.when(slot < count[0, 0])
    def _():
        left_high, left_low = halves(left[0])
        inner = product(left_high, left_low, field_high[...], field_low[...])
        inner_high, inner_low = halves(inner)
        right_high, right_low = halves(right[0])
        result = product(inner_high, inner_low, right_high, right_low)
        goal = target[0, slot]
        kept = goal == sector
        swapped_here = goal == (sector ^ 1)
        roles = (jnp.logical_not(kept | swapped_here), kept, swapped_here)
        for role, out in zip(roles, outs):

            @pl.when(role)
            def _(out=out):
                out[...] += result


def first_kernel(count, target, left, right, field, crossing, kept, local, f_high, f_low):
    @pl.when(pl.program_id(0) == 0)
    def _():
        f_high[...], f_low[...] = halves(field[...])

    outs = (crossing, kept, local)
    accumulate(lax.axis_index(SECTOR), count, target, left, right, f_high, f_low, outs)


def second_kernel(
    count, target, left, right, sums, field, gathered, crossing, kept, local, overlap, f_high, f_low
):
    peers, slab, width = field.shape

    @pl.when(pl.program_id(0) == 0)
    def _():
        rayleigh = sums[0:1, 0:1] / sums[1:2, 0:1]
        weighted = jnp.zeros((slab, width), F32)
        for peer in range(peers):
            vector = field[peer]
            raw = gathered[peer, slab:] * (gathered[peer, :slab] - rayleigh * vector)
            f_high[peer], f_low[peer] = halves(raw)
            weighted += vector * raw
        overlap[...] = jnp.broadcast_to(jnp.sum(weighted, keepdims=True), overlap.shape)

    outs = (crossing, kept, local)
    flat = (peers * slab, width)
    f_high, f_low = f_high.reshape(flat), f_low.reshape(flat)
    accumulate(lax.axis_index(SECTOR), count, target, left, right, f_high, f_low, outs)


def partial_image(body, counts, targets, left_stack, right_stack, fields, extra=(), scratch=None, streamed=False):
    slots, width, _ = right_stack.shape

    def operand(i, count):
        return (jnp.minimum(i, count[0, 0] - 1), 0, 0)

    in_vmem = pl.BlockSpec(memory_space=pltpu.VMEM)
    targets, left_stack, right_stack = (
        pltpu.with_memory_space_constraint(x, pltpu.HBM)
        for x in (targets, left_stack, right_stack)
    )
    block = (width, width)
    field_spec = in_vmem
    if streamed:
        fields = [pltpu.with_memory_space_constraint(x, pltpu.HBM) for x in fields]
        field_spec = pl.BlockSpec(block, lambda i, *_: (0, 0), pipeline_mode=pl.Buffered(1))
    return pl.pallas_call(
        body,
        out_shape=[jax.ShapeDtypeStruct(x, F32) for x in (*[block] * 3, *extra)],
        grid_spec=pltpu.PrefetchScalarGridSpec(
            num_scalar_prefetch=1,
            grid=(slots,),
            in_specs=[
                pl.BlockSpec(targets.shape, lambda i, *_: (0, 0), memory_space=pltpu.SMEM),
                pl.BlockSpec((1, width, width), operand),
                pl.BlockSpec((1, width, width), operand),
                *[field_spec] * len(fields),
            ],
            out_specs=[in_vmem] * (3 + len(extra)),
            scratch_shapes=[pltpu.VMEM(scratch or block, jnp.bfloat16)] * 2,
        ),
        compiler_params=pltpu.CompilerParams(
            dimension_semantics=("arbitrary",), vmem_limit_bytes=KERNEL_VMEM
        ),
        cost_estimate=pl.CostEstimate(
            flops=slots * 12 * width**3, bytes_accessed=slots * 8 * width**2, transcendentals=0
        ),
    )(counts, targets, left_stack, right_stack, *fields)


def tiles(x, slab, width):
    return [(c * slab, slice(c * LANES, (c + 1) * LANES)) for c in range(width // LANES)]


def combine_kernel(mid, crossed, local, field, packed, sums):
    peers, slab, width = mid.shape
    where = tiles(mid, slab, width)
    cross = jnp.zeros((slab, width), F32)
    for peer in range(peers):
        total = mid[peer] + (crossed[peer] + local[peer])
        for row, lanes in where:
            packed[peer, row : row + slab] = total[:, lanes]
        cross += field[peer] * total
    own = field[lax.axis_index(TERM)]
    line = lax.broadcasted_iota(jnp.int32, (EXTRA, LANES), 0)
    sums[...] = jnp.where(
        line == 0, jnp.sum(cross, keepdims=True), jnp.sum(own * own, keepdims=True)
    )
    for peer in range(peers):
        packed[peer, len(where) * slab :] = sums[...]


def gathered_kernel(arrived, scaling, image, copies, sums):
    peers = copies.shape[0]
    slab, width = image.shape
    total = arrived[0]
    for peer in range(1, peers):
        total += arrived[peer]
    where = tiles(image, slab, width)
    for row, lanes in where:
        image[:, lanes] = total[row : row + slab]
    for peer in range(peers):
        copies[peer, :slab] = image[...]
        copies[peer, slab:] = scaling[...]
    sums[...] = total[len(where) * slab :]


def small_call(body, out_shapes, args, scratch=(), spaces=None):
    spaces = spaces or [pltpu.VMEM] * len(out_shapes)
    return pl.pallas_call(
        body,
        in_specs=[pl.BlockSpec(memory_space=pltpu.VMEM)] * len(args),
        out_specs=[
            pl.BlockSpec() if space == pltpu.HBM else pl.BlockSpec(memory_space=space)
            for space in spaces
        ],
        out_shape=[
            pltpu.HBM(s, F32) if space == pltpu.HBM else jax.ShapeDtypeStruct(s, F32)
            for s, space in zip(out_shapes, spaces)
        ],
        scratch_shapes=scratch,
        compiler_params=pltpu.CompilerParams(vmem_limit_bytes=32 * MIB),
    )(*args)


def per_device(wavefunction, precond, left_ops, right_ops, out_sector, live_counts):
    peers = lax.axis_size(TERM)
    width = wavefunction.shape[1]
    slab = width // peers
    split = (peers, slab, width)
    packed_rows = slab * (width // LANES) + EXTRA
    field = wavefunction[0]
    scaling = precond[0]
    image_of = functools.partial(
        partial_image,
        counts=live_counts,
        targets=out_sector,
        left_stack=left_ops[0],
        right_stack=right_ops[0],
    )

    crossing, mid, local = image_of(first_kernel, fields=(field,), streamed=True)
    crossed, local = moved(crossing, local)
    (packed,) = small_call(
        combine_kernel,
        [(peers, packed_rows, LANES)],
        [x.reshape(split) for x in (mid, crossed, local, field)],
        [pltpu.VMEM((EXTRA, LANES), F32)],
    )
    first_image, copies, sums = small_call(
        gathered_kernel,
        [(slab, width), (peers, 2 * slab, width), (EXTRA, LANES)],
        [swapped(packed), scaling],
        spaces=[pltpu.VMEM, pltpu.HBM, pltpu.VMEM],
    )
    gathered = swapped(copies)
    sums = over_sectors(sums)

    fields = (sums, field.reshape(split), gathered)
    crossing, mid, local, overlap = image_of(
        second_kernel, fields=fields, extra=[(EXTRA, LANES)], scratch=split
    )
    crossed, local = moved(crossing, local)
    overlap = over_sectors(overlap, slice(0, 2))
    crossed, overlap = lax.optimization_barrier((crossed, overlap))
    total = mid + crossed + local
    overlap = over_sectors(overlap, slice(2, None))
    arrived = swapped(total.reshape(split))

    norm_sq = sums[1:2, 0:1]
    rayleigh = sums[0:1, 0:1] / norm_sq
    share = overlap[0:1, 0:1] / norm_sq
    own = lax.dynamic_index_in_dim(
        field.reshape(split), lax.axis_index(TERM), 0, keepdims=False
    )
    correction = scaling * (first_image - rayleigh * own) - share * own
    second_image = arrived.sum(axis=0) - share * first_image
    return (first_image[None], correction[None], second_image[None])


def solution(mesh):
    torus = Mesh(mesh.devices.reshape(4, 4, 8, 2), ("term_0", "term_1", "sector_0", "sector_1"))
    placed = (
        P(SECTOR, None, None),
        P(SECTOR, TERM, None),
        P(SECTOR, TERM, None, None),
        P(SECTOR, TERM, None, None),
        P(SECTOR, TERM),
        P(SECTOR, TERM),
    )
    return jax.shard_map(
        per_device,
        mesh=torus,
        in_specs=placed,
        out_specs=(P(SECTOR, TERM, None), P(SECTOR, TERM, None), P(SECTOR, TERM, None)),
        check_vma=False,
    )
```

```python
import functools

import jax
import jax.numpy as jnp
from jax import lax
from jax.experimental import pallas as pl
from jax.experimental.pallas import tpu as pltpu
from jax.sharding import Mesh
from jax.sharding import PartitionSpec as P

TERM = ("term_0", "term_1")
SECTOR = ("sector_0", "sector_1")
LANES = 128
EXTRA = 8
HALVES = 2
MIB = 1 << 20
KERNEL_VMEM = 20 * MIB
F32 = jnp.float32


def moved(crossing, local):
    count = lax.axis_size(SECTOR)
    upward = [(i, i + 1) for i in range(1, count - 1, 2)]
    downward = [(j, i) for i, j in upward]
    swap = [(i, i ^ 1) for i in range(count)]
    return lax.ppermute(crossing, SECTOR, upward + downward), lax.ppermute(local, SECTOR, swap)


def rotated(x):
    terms, sectors = lax.axis_size(TERM), lax.axis_size(SECTOR)
    pairs = [
        (t * sectors + (s + t) % sectors, t * sectors + s)
        for t in range(terms)
        for s in range(sectors)
    ]
    return lax.ppermute(x, (*TERM, *SECTOR), pairs)


def exchanged_along(pieces, axis):
    size = len(pieces)
    routes = [[(i, (i + k) % size) for i in range(size)] for k in range(size)]
    sent = [lax.ppermute(pieces[k], axis, routes[k]) for k in range(1, size)]
    return [pieces[0], *sent]


def swapped(x):
    return lax.all_to_all(x, TERM, 0, 0, tiled=True)


def sector_steps():
    for axis in SECTOR[::-1]:
        count = lax.axis_size(axis)
        mask = 1
        while mask < count:
            yield functools.partial(exchanged, axis=axis, mask=mask)
            mask *= 2


def exchanged(x, axis, mask):
    pairs = [(i, i ^ mask) for i in range(lax.axis_size(axis))]
    return x + lax.ppermute(x, axis, pairs)


def over_sectors(x):
    for step in sector_steps():
        x = step(x)
    return x


def halves(x):
    high = x.astype(jnp.bfloat16)
    low = (x - high.astype(F32)).astype(jnp.bfloat16)
    return high, low


def product(a_high, a_low, b_high, b_low):
    dot = functools.partial(jnp.dot, preferred_element_type=F32)
    return dot(a_high, b_high) + (dot(a_high, b_low) + dot(a_low, b_high))


def accumulate(sector, count, target, left, right, field_high, field_low, outs):
    slot = pl.program_id(0)

    @pl.when(slot == 0)
    def _():
        for out in outs:
            out[...] = jnp.zeros_like(out)

    peers, rows, width = outs[0].shape

    @pl.when(slot < count[0, 0])
    def _():
        left_high, left_low = halves(left[0])
        inner = product(left_high, left_low, field_high[...], field_low[...])
        inner_high, inner_low = halves(inner)
        right_high, right_low = halves(right[0])
        result = product(inner_high, inner_low, right_high, right_low)
        goal = target[0, slot]
        kept = goal == sector
        swapped_here = goal == (sector ^ 1)
        roles = (jnp.logical_not(kept | swapped_here), kept, swapped_here)
        result = result.reshape(peers, HALVES * rows, width)
        for i, role in enumerate(roles):

            @pl.when(role)
            def _(i=i):
                for half in range(HALVES):
                    outs[i * HALVES + half][...] += result[:, half * rows : (half + 1) * rows]


def first_kernel(count, target, left, right, field, *rest):
    *outs, f_high, f_low = rest

    @pl.when(pl.program_id(0) == 0)
    def _():
        f_high[...], f_low[...] = halves(field[...])

    accumulate(lax.axis_index(SECTOR), count, target, left, right, f_high, f_low, outs)


def second_kernel(count, target, left, right, sums, field, gathered, *rest):
    *outs, overlap, f_high, f_low = rest
    peers, slab, width = field.shape

    @pl.when(pl.program_id(0) == 0)
    def _():
        rayleigh = sums[0:1, 0:1] / sums[1:2, 0:1]
        weighted = jnp.zeros((slab, width), F32)
        for peer in range(peers):
            vector = field[peer]
            raw = gathered[peer, slab:] * (gathered[peer, :slab] - rayleigh * vector)
            f_high[peer], f_low[peer] = halves(raw)
            weighted += vector * raw
        overlap[...] = jnp.broadcast_to(jnp.sum(weighted, keepdims=True), overlap.shape)

    flat = (peers * slab, width)
    f_high, f_low = f_high.reshape(flat), f_low.reshape(flat)
    accumulate(lax.axis_index(SECTOR), count, target, left, right, f_high, f_low, outs)


def partial_image(body, counts, targets, left_stack, right_stack, fields, split, extra=(), scratch=None, streamed=False):
    slots, width, _ = right_stack.shape

    def operand(i, count):
        return (jnp.minimum(i, count[0, 0] - 1), 0, 0)

    in_vmem = pl.BlockSpec(memory_space=pltpu.VMEM)
    targets, left_stack, right_stack = (
        pltpu.with_memory_space_constraint(x, pltpu.HBM)
        for x in (targets, left_stack, right_stack)
    )
    block = (width, width)
    part = (split[0], split[1] // HALVES, width)
    parts = 3 * HALVES
    field_spec = in_vmem
    if streamed:
        fields = [pltpu.with_memory_space_constraint(x, pltpu.HBM) for x in fields]
        field_spec = pl.BlockSpec(block, lambda i, *_: (0, 0), pipeline_mode=pl.Buffered(1))
    return pl.pallas_call(
        body,
        out_shape=[jax.ShapeDtypeStruct(x, F32) for x in (*[part] * parts, *extra)],
        grid_spec=pltpu.PrefetchScalarGridSpec(
            num_scalar_prefetch=1,
            grid=(slots,),
            in_specs=[
                pl.BlockSpec(targets.shape, lambda i, *_: (0, 0), memory_space=pltpu.SMEM),
                pl.BlockSpec((1, width, width), operand),
                pl.BlockSpec((1, width, width), operand),
                *[field_spec] * len(fields),
            ],
            out_specs=[in_vmem] * (parts + len(extra)),
            scratch_shapes=[pltpu.VMEM(scratch or block, jnp.bfloat16)] * 2,
        ),
        compiler_params=pltpu.CompilerParams(
            dimension_semantics=("arbitrary",), vmem_limit_bytes=KERNEL_VMEM
        ),
        cost_estimate=pl.CostEstimate(
            flops=slots * 12 * width**3, bytes_accessed=slots * 8 * width**2, transcendentals=0
        ),
    )(counts, targets, left_stack, right_stack, *fields)


def place(half, along, across, size):
    return along * size + across if half == 0 else across * size + along


def spread(half, pieces, kept, crossed, local, weight=None):
    peers, rows, width = kept.shape
    size = len(pieces)
    me = lax.axis_index(TERM[half])
    weighted = jnp.zeros((rows, width), F32)
    for k, piece in enumerate(pieces):
        for across in range(size):
            peer = place(half, lax.rem(me + k, size), across, size)
            total = kept[peer] + (crossed[peer] + local[peer])
            piece[across * rows : (across + 1) * rows] = total
            if weight is not None:
                weighted += weight[peer, half * rows : (half + 1) * rows] * total
    return weighted


def first_spread(half, kept, crossed, local, field, *rest):
    *pieces, tail = rest
    rows = kept.shape[1]
    cross = spread(half, pieces, kept, crossed, local, field)
    own = field[lax.axis_index(TERM), half * rows : (half + 1) * rows]
    line = lax.broadcasted_iota(jnp.int32, tail.shape, 0)
    tail[...] = jnp.where(
        line == 0, jnp.sum(cross, keepdims=True), jnp.sum(own * own, keepdims=True)
    )
    for piece in pieces:
        piece[len(pieces) * rows :] = tail[...]


def second_spread(half, kept, crossed, local, *rest):
    if half == 0:
        spread(half, rest, kept, crossed, local)
        return
    tail, *pieces = rest
    spread(half, pieces, kept, crossed, local)
    lanes = tail.shape[1]
    for piece in pieces:
        for start in range(0, piece.shape[1], lanes):
            piece[len(pieces) * kept.shape[1] :, start : start + lanes] = tail[...]


def relay(axis, rows, *refs):
    size = len(refs) // 2
    arrived, pieces = refs[:size], refs[size:]
    me = lax.axis_index(axis)

    def summed(where):
        return functools.reduce(lambda x, y: x + y, [ref[where] for ref in arrived])

    for k, piece in enumerate(pieces):
        start = pl.multiple_of(lax.rem(me + k, size) * rows, rows)
        piece[:rows] = summed(pl.ds(start, rows))
        if piece.shape[0] > rows:
            piece[rows:] = summed(pl.ds(size * rows, piece.shape[0] - rows))


def landed(refs, rows):
    size = len(refs) // HALVES
    groups = [refs[h * size : (h + 1) * size] for h in range(HALVES)]
    totals = [functools.reduce(lambda x, y: x + y, [r[...] for r in g]) for g in groups]
    tails = [t[rows:] for t in totals if t.shape[0] > rows]
    return [t[:rows] for t in totals], functools.reduce(lambda x, y: x + y, tails)


def first_landing(*refs):
    *arrived, scaling, image, copies, sums = refs
    peers, slab = copies.shape[0], image.shape[0]
    rows = slab // HALVES
    parts, tail = landed(arrived, rows)
    for half, part in enumerate(parts):
        image[half * rows : (half + 1) * rows] = part
    for peer in range(peers):
        copies[peer, :slab] = image[...]
        copies[peer, slab:] = scaling[...]
    sums[...] = tail[:, : sums.shape[1]]


def second_landing(*refs):
    *arrived, sums, first_image, scaling, own, correction, image = refs
    rows = image.shape[0] // HALVES
    parts, tail = landed(arrived, rows)
    rayleigh = sums[0:1, 0:1] / sums[1:2, 0:1]
    share = tail[0:1, 0:1] / sums[1:2, 0:1]
    vector = own[...]
    correction[...] = scaling[...] * (first_image[...] - rayleigh * vector) - share * vector
    for half, part in enumerate(parts):
        lines = slice(half * rows, (half + 1) * rows)
        image[lines] = part - share * first_image[lines]


def relayed(half, pieces, rows):
    arrived = exchanged_along(pieces, TERM[half])
    other = TERM[1 - half]
    shape = (rows + pieces[0].shape[0] - len(pieces) * rows, pieces[0].shape[1])
    onward = small_call(
        functools.partial(relay, other, rows), [shape] * len(pieces), arrived
    )
    return exchanged_along(onward, other)


def small_call(body, out_shapes, args, scratch=(), spaces=None):
    spaces = spaces or [pltpu.VMEM] * len(out_shapes)
    return pl.pallas_call(
        body,
        in_specs=[pl.BlockSpec(memory_space=pltpu.VMEM)] * len(args),
        out_specs=[
            pl.BlockSpec() if space == pltpu.HBM else pl.BlockSpec(memory_space=space)
            for space in spaces
        ],
        out_shape=[
            pltpu.HBM(s, F32) if space == pltpu.HBM else jax.ShapeDtypeStruct(s, F32)
            for s, space in zip(out_shapes, spaces)
        ],
        scratch_shapes=scratch,
        compiler_params=pltpu.CompilerParams(vmem_limit_bytes=32 * MIB),
    )(*args)


def per_device(wavefunction, precond, left_ops, right_ops, out_sector, live_counts):
    peers = lax.axis_size(TERM)
    width = wavefunction.shape[1]
    slab = width // peers
    split = (peers, slab, width)
    rows = slab // HALVES
    size = lax.axis_size(TERM[0])
    field = wavefunction[0]
    blocked = field.reshape(split)
    scaling = precond[0]
    image_of = functools.partial(
        partial_image,
        counts=live_counts,
        targets=out_sector,
        left_stack=left_ops[0],
        right_stack=right_ops[0],
        split=split,
    )

    def moved_parts(parts):
        crossing, kept, local = (parts[i * HALVES : (i + 1) * HALVES] for i in range(3))
        return [(k, *moved(c, l)) for c, k, l in zip(crossing, kept, local)]

    parts = moved_parts(image_of(first_kernel, fields=(field,), streamed=True))
    arrived = []
    for half in range(HALVES):
        pieces = small_call(
            functools.partial(first_spread, half),
            [(size * rows + EXTRA, width)] * size,
            [*parts[half], blocked],
            [pltpu.VMEM((EXTRA, width), F32)],
        )
        arrived += relayed(half, pieces, rows)
    first_image, copies, sums = small_call(
        first_landing,
        [(slab, width), (peers, 2 * slab, width), (EXTRA, LANES)],
        [*arrived, scaling],
        spaces=[pltpu.VMEM, pltpu.HBM, pltpu.VMEM],
    )
    gathered = swapped(copies)
    sums = over_sectors(sums)

    *parts, overlap = image_of(
        second_kernel, fields=(sums, blocked, gathered), extra=[(EXTRA, LANES)], scratch=split
    )
    parts = moved_parts(parts)
    overlap = rotated(overlap)
    arrived = []
    for half in range(HALVES):
        tail = [overlap] if half else []
        pieces = small_call(
            functools.partial(second_spread, half),
            [(size * rows + EXTRA * half, width)] * size,
            [*parts[half], *tail],
        )
        arrived += relayed(half, pieces, rows)
    own = lax.dynamic_index_in_dim(blocked, lax.axis_index(TERM), 0, keepdims=False)
    correction, second_image = small_call(
        second_landing,
        [(slab, width)] * 2,
        [*arrived, sums, first_image, scaling, own],
    )
    return (first_image[None], correction[None], second_image[None])


def solution(mesh):
    torus = Mesh(mesh.devices.reshape(4, 4, 8, 2), ("term_0", "term_1", "sector_0", "sector_1"))
    placed = (
        P(SECTOR, None, None),
        P(SECTOR, TERM, None),
        P(SECTOR, TERM, None, None),
        P(SECTOR, TERM, None, None),
        P(SECTOR, TERM),
        P(SECTOR, TERM),
    )
    return jax.shard_map(
        per_device,
        mesh=torus,
        in_specs=placed,
        out_specs=(P(SECTOR, TERM, None), P(SECTOR, TERM, None), P(SECTOR, TERM, None)),
        check_vma=False,
    )
```

```python
import functools

import jax
import jax.numpy as jnp
from jax import lax
from jax.experimental import pallas as pl
from jax.experimental.pallas import tpu as pltpu
from jax.sharding import Mesh
from jax.sharding import PartitionSpec as P

TERM = ("term_0", "term_1")
SECTOR = ("sector_0", "sector_1")
LANES = 128
EXTRA = 8
HALVES = 2
MIB = 1 << 20
KERNEL_VMEM = 20 * MIB
F32 = jnp.float32


def moved(crossing, local):
    count = lax.axis_size(SECTOR)
    upward = [(i, i + 1) for i in range(1, count - 1, 2)]
    downward = [(j, i) for i, j in upward]
    swap = [(i, i ^ 1) for i in range(count)]
    return lax.ppermute(crossing, SECTOR, upward + downward), lax.ppermute(local, SECTOR, swap)


def rotated(x):
    terms, sectors = lax.axis_size(TERM), lax.axis_size(SECTOR)
    pairs = [
        (t * sectors + (s + t) % sectors, t * sectors + s)
        for t in range(terms)
        for s in range(sectors)
    ]
    return lax.ppermute(x, (*TERM, *SECTOR), pairs)


def exchanged_along(pieces, axis):
    size = len(pieces)
    routes = [[(i, (i + k) % size) for i in range(size)] for k in range(size)]
    sent = [lax.ppermute(pieces[k], axis, routes[k]) for k in range(1, size)]
    return [pieces[0], *sent]


def copied_along(piece, axis):
    size = lax.axis_size(axis)
    routes = [[(i, (i + k) % size) for i in range(size)] for k in range(size)]
    return [piece, *[lax.ppermute(piece, axis, route) for route in routes[1:]]]


def halves(x):
    high = x.astype(jnp.bfloat16)
    low = (x - high.astype(F32)).astype(jnp.bfloat16)
    return high, low


def product(a_high, a_low, b_high, b_low):
    dot = functools.partial(jnp.dot, preferred_element_type=F32)
    return dot(a_high, b_high) + (dot(a_high, b_low) + dot(a_low, b_high))


def accumulate(sector, count, target, left, right, field_high, field_low, outs):
    slot = pl.program_id(0)

    @pl.when(slot == 0)
    def _():
        for out in outs:
            out[...] = jnp.zeros_like(out)

    peers, rows, width = outs[0].shape

    @pl.when(slot < count[0, 0])
    def _():
        left_high, left_low = halves(left[0])
        inner = product(left_high, left_low, field_high[...], field_low[...])
        inner_high, inner_low = halves(inner)
        right_high, right_low = halves(right[0])
        result = product(inner_high, inner_low, right_high, right_low)
        goal = target[0, slot]
        kept = goal == sector
        swapped_here = goal == (sector ^ 1)
        roles = (jnp.logical_not(kept | swapped_here), kept, swapped_here)
        result = result.reshape(peers, HALVES * rows, width)
        for i, role in enumerate(roles):

            @pl.when(role)
            def _(i=i):
                for half in range(HALVES):
                    outs[i * HALVES + half][...] += result[:, half * rows : (half + 1) * rows]


def first_kernel(count, target, left, right, field, *rest):
    *outs, f_high, f_low = rest

    @pl.when(pl.program_id(0) == 0)
    def _():
        f_high[...], f_low[...] = halves(field[...])

    accumulate(lax.axis_index(SECTOR), count, target, left, right, f_high, f_low, outs)


def second_kernel(count, target, left, right, field, *rest):
    *rings, tile, f_high, f_low = rest
    outs = rings[-3 * HALVES :]
    rings = rings[: -3 * HALVES]
    peers, slab, width = field.shape
    rows = slab // HALVES

    @pl.when(pl.program_id(0) == 0)
    def _():
        size = len(rings) // HALVES
        tails = [ring[k, 2 * rows :] for ring in rings[size:] for k in range(size)]
        sums = functools.reduce(lambda x, y: x + y, tails)
        rayleigh = sums[0:1, 0:1] / sums[1:2, 0:1]
        weighted = jnp.zeros((rows, width), F32)
        for half in range(HALVES):
            lines = slice(half * rows, (half + 1) * rows)
            first, last = (lax.axis_index(TERM[i]) for i in (1 - half, half))
            for j, ring in enumerate(rings[half * size : (half + 1) * size]):
                for k in range(size):
                    along = lax.rem(last + size - j, size)
                    peer = place(half, along, lax.rem(first + size - k, size), size)
                    vector = field[peer, lines]
                    image, scaling = ring[k, :rows], ring[k, rows : 2 * rows]
                    raw = scaling * (image - rayleigh * vector)
                    f_high[peer, lines], f_low[peer, lines] = halves(raw)
                    weighted += vector * raw
        line = lax.broadcasted_iota(jnp.int32, tile.shape, 0)
        overlap = jnp.sum(weighted, keepdims=True)
        tile[...] = jnp.where(line == 2, overlap, sums[:, : tile.shape[1]])

    flat = (peers * slab, width)
    f_high, f_low = f_high.reshape(flat), f_low.reshape(flat)
    accumulate(lax.axis_index(SECTOR), count, target, left, right, f_high, f_low, outs)


def partial_image(body, counts, targets, left_stack, right_stack, fields, split, extra=(), scratch=None, streamed=False):
    slots, width, _ = right_stack.shape

    def operand(i, count):
        return (jnp.minimum(i, count[0, 0] - 1), 0, 0)

    in_vmem = pl.BlockSpec(memory_space=pltpu.VMEM)
    targets, left_stack, right_stack = (
        pltpu.with_memory_space_constraint(x, pltpu.HBM)
        for x in (targets, left_stack, right_stack)
    )
    block = (width, width)
    part = (split[0], split[1] // HALVES, width)
    parts = 3 * HALVES
    field_spec = in_vmem
    if streamed:
        fields = [pltpu.with_memory_space_constraint(x, pltpu.HBM) for x in fields]
        field_spec = pl.BlockSpec(block, lambda i, *_: (0, 0), pipeline_mode=pl.Buffered(1))
    return pl.pallas_call(
        body,
        out_shape=[jax.ShapeDtypeStruct(x, F32) for x in (*[part] * parts, *extra)],
        grid_spec=pltpu.PrefetchScalarGridSpec(
            num_scalar_prefetch=1,
            grid=(slots,),
            in_specs=[
                pl.BlockSpec(targets.shape, lambda i, *_: (0, 0), memory_space=pltpu.SMEM),
                pl.BlockSpec((1, width, width), operand),
                pl.BlockSpec((1, width, width), operand),
                *[field_spec] * len(fields),
            ],
            out_specs=[in_vmem] * (parts + len(extra)),
            scratch_shapes=[pltpu.VMEM(scratch or block, jnp.bfloat16)] * 2,
        ),
        compiler_params=pltpu.CompilerParams(
            dimension_semantics=("arbitrary",), vmem_limit_bytes=KERNEL_VMEM
        ),
        cost_estimate=pl.CostEstimate(
            flops=slots * 12 * width**3, bytes_accessed=slots * 8 * width**2, transcendentals=0
        ),
    )(counts, targets, left_stack, right_stack, *fields)


def place(half, along, across, size):
    return along * size + across if half == 0 else across * size + along


def spread(half, pieces, kept, crossed, local, weight=None):
    peers, rows, width = kept.shape
    size = len(pieces)
    me = lax.axis_index(TERM[half])
    weighted = jnp.zeros((rows, width), F32)
    for k, piece in enumerate(pieces):
        for across in range(size):
            peer = place(half, lax.rem(me + k, size), across, size)
            total = kept[peer] + (crossed[peer] + local[peer])
            piece[across * rows : (across + 1) * rows] = total
            if weight is not None:
                weighted += weight[peer, half * rows : (half + 1) * rows] * total
    return weighted


def first_spread(half, kept, crossed, local, field, *rest):
    *pieces, tail = rest
    rows = kept.shape[1]
    cross = spread(half, pieces, kept, crossed, local, field)
    own = field[lax.axis_index(TERM), half * rows : (half + 1) * rows]
    line = lax.broadcasted_iota(jnp.int32, tail.shape, 0)
    tail[...] = jnp.where(
        line == 0, jnp.sum(cross, keepdims=True), jnp.sum(own * own, keepdims=True)
    )
    for piece in pieces:
        piece[len(pieces) * rows :] = tail[...]


def second_spread(half, kept, crossed, local, *rest):
    if half == 0:
        spread(half, rest, kept, crossed, local)
        return
    tail, *pieces = rest
    spread(half, pieces, kept, crossed, local)
    lanes = tail.shape[1]
    for piece in pieces:
        for start in range(0, piece.shape[1], lanes):
            piece[len(pieces) * kept.shape[1] :, start : start + lanes] = tail[...]


def relay(axis, rows, *refs):
    size = len(refs) // 2
    arrived, pieces = refs[:size], refs[size:]
    me = lax.axis_index(axis)

    def summed(where):
        return functools.reduce(lambda x, y: x + y, [ref[where] for ref in arrived])

    for k, piece in enumerate(pieces):
        start = pl.multiple_of(lax.rem(me + k, size) * rows, rows)
        piece[:rows] = summed(pl.ds(start, rows))
        if piece.shape[0] > rows:
            piece[rows:] = summed(pl.ds(size * rows, piece.shape[0] - rows))


def added(refs):
    return functools.reduce(lambda x, y: x + y, [ref[...] for ref in refs])


def first_landing(*refs):
    *arrived, scaling, first, last, piece, tile = refs
    rows = first.shape[0]
    size = len(arrived) // HALVES
    totals = [added(arrived[h * size : (h + 1) * size]) for h in range(HALVES)]
    first[...] = totals[0][:rows]
    last[...] = totals[1][:rows]
    piece[:rows] = totals[0][:rows]
    piece[rows:] = scaling[:rows]
    tile[...] = (totals[0] + totals[1])[rows:, : tile.shape[1]]


def tailed(image, scaling, tile, piece):
    rows, width = image.shape
    piece[:rows] = image[...]
    piece[rows : 2 * rows] = scaling[rows:]
    for start in range(0, width, tile.shape[1]):
        piece[2 * rows :, start : start + tile.shape[1]] = tile[...]


def stacked(*refs):
    pieces, stacks = refs[:-HALVES], refs[-HALVES:]
    size = len(pieces) // HALVES
    for i, piece in enumerate(pieces):
        stacks[i // size][i % size] = piece[...]


def second_landing(*refs):
    *arrived, sums, first, last, scaling, own, correction, image = refs
    rows = first.shape[0]
    size = len(arrived) // HALVES
    totals = [added(arrived[h * size : (h + 1) * size]) for h in range(HALVES)]
    rayleigh = sums[0:1, 0:1] / sums[1:2, 0:1]
    share = totals[-1][rows + 2 : rows + 3, 0:1] / sums[1:2, 0:1]
    for half, part in enumerate((first, last)):
        lines = slice(half * rows, (half + 1) * rows)
        vector = own[lines]
        raw = scaling[lines] * (part[...] - rayleigh * vector)
        correction[lines] = raw - share * vector
        image[lines] = totals[half][:rows] - share * part[...]


def gathered(ends):
    pieces = [copied_along(x, TERM[1 - half]) for half, x in enumerate(ends)]
    shapes = [(len(p), *x.shape) for p, x in zip(pieces, ends)]
    stacks = small_call(stacked, shapes, sum(pieces, []))
    return sum((copied_along(x, TERM[half]) for half, x in enumerate(stacks)), [])


def relayed(half, pieces, rows):
    arrived = exchanged_along(pieces, TERM[half])
    other = TERM[1 - half]
    shape = (rows + pieces[0].shape[0] - len(pieces) * rows, pieces[0].shape[1])
    onward = small_call(
        functools.partial(relay, other, rows), [shape] * len(pieces), arrived
    )
    return exchanged_along(onward, other)


def small_call(body, out_shapes, args, scratch=()):
    in_vmem = pl.BlockSpec(memory_space=pltpu.VMEM)
    return pl.pallas_call(
        body,
        in_specs=[in_vmem] * len(args),
        out_specs=[in_vmem] * len(out_shapes),
        out_shape=[jax.ShapeDtypeStruct(s, F32) for s in out_shapes],
        scratch_shapes=scratch,
        compiler_params=pltpu.CompilerParams(vmem_limit_bytes=32 * MIB),
    )(*args)


def per_device(wavefunction, precond, left_ops, right_ops, out_sector, live_counts):
    peers = lax.axis_size(TERM)
    width = wavefunction.shape[1]
    slab = width // peers
    split = (peers, slab, width)
    rows = slab // HALVES
    size = lax.axis_size(TERM[0])
    field = wavefunction[0]
    blocked = field.reshape(split)
    scaling = precond[0]
    image_of = functools.partial(
        partial_image,
        counts=live_counts,
        targets=out_sector,
        left_stack=left_ops[0],
        right_stack=right_ops[0],
        split=split,
    )

    def moved_parts(parts):
        crossing, kept, local = (parts[i * HALVES : (i + 1) * HALVES] for i in range(3))
        return [(k, *moved(c, l)) for c, k, l in zip(crossing, kept, local)]

    parts = moved_parts(image_of(first_kernel, fields=(field,), streamed=True))
    arrived = []
    for half in range(HALVES):
        pieces = small_call(
            functools.partial(first_spread, half),
            [(size * rows + EXTRA, width)] * size,
            [*parts[half], blocked],
            [pltpu.VMEM((EXTRA, width), F32)],
        )
        arrived += relayed(half, pieces, rows)
    part, tile = (rows, width), (EXTRA, LANES)
    first, last, end, sums = small_call(
        first_landing, [part, part, (2 * rows, width), tile], [*arrived, scaling]
    )
    (tailed_end,) = small_call(
        tailed, [(2 * rows + EXTRA, width)], [last, scaling, rotated(sums)]
    )
    rings = gathered([end, tailed_end])

    *parts, sums = image_of(
        second_kernel, fields=(blocked, *rings), extra=[tile], scratch=split
    )
    parts = moved_parts(parts)
    overlap = rotated(sums)
    arrived = []
    for half in range(HALVES):
        tail = [overlap] if half else []
        pieces = small_call(
            functools.partial(second_spread, half),
            [(size * rows + EXTRA * half, width)] * size,
            [*parts[half], *tail],
        )
        arrived += relayed(half, pieces, rows)
    own = lax.dynamic_index_in_dim(blocked, lax.axis_index(TERM), 0, keepdims=False)
    correction, second_image = small_call(
        second_landing,
        [(slab, width)] * 2,
        [*arrived, sums, first, last, scaling, own],
    )
    first_image = jnp.concatenate([first, last], axis=0)
    return (first_image[None], correction[None], second_image[None])


def solution(mesh):
    torus = Mesh(mesh.devices.reshape(4, 4, 8, 2), ("term_0", "term_1", "sector_0", "sector_1"))
    placed = (
        P(SECTOR, None, None),
        P(SECTOR, TERM, None),
        P(SECTOR, TERM, None, None),
        P(SECTOR, TERM, None, None),
        P(SECTOR, TERM),
        P(SECTOR, TERM),
    )
    return jax.shard_map(
        per_device,
        mesh=torus,
        in_specs=placed,
        out_specs=(P(SECTOR, TERM, None), P(SECTOR, TERM, None), P(SECTOR, TERM, None)),
        check_vma=False,
    )
```

```python
import functools

import jax
import jax.numpy as jnp
from jax import lax
from jax.experimental import pallas as pl
from jax.experimental.pallas import tpu as pltpu
from jax.sharding import Mesh
from jax.sharding import PartitionSpec as P

TERM = ("term_0", "term_1")
SECTOR = ("sector_0", "sector_1")
LANES = 128
EXTRA = 8
HALVES = 2
MIB = 1 << 20
KERNEL_VMEM = 18 * MIB
SMALL_VMEM = 8 * MIB
F32 = jnp.float32


def moved(crossing, local):
    count = lax.axis_size(SECTOR)
    upward = [(i, i + 1) for i in range(1, count - 1, 2)]
    downward = [(j, i) for i, j in upward]
    swap = [(i, i ^ 1) for i in range(count)]
    return lax.ppermute(crossing, SECTOR, upward + downward), lax.ppermute(local, SECTOR, swap)


def exchanged_along(pieces, axis):
    size = len(pieces)
    routes = [[(i, (i + k) % size) for i in range(size)] for k in range(size)]
    sent = [lax.ppermute(pieces[k], axis, routes[k]) for k in range(1, size)]
    return [pieces[0], *sent]


def swapped(x):
    return lax.all_to_all(x, TERM, 0, 0, tiled=True)


def sector_steps():
    for axis in SECTOR[::-1]:
        count = lax.axis_size(axis)
        mask = 1
        while mask < count:
            yield functools.partial(exchanged, axis=axis, mask=mask)
            mask *= 2


def exchanged(x, axis, mask):
    pairs = [(i, i ^ mask) for i in range(lax.axis_size(axis))]
    return x + lax.ppermute(x, axis, pairs)


def over_sectors(x):
    for step in sector_steps():
        x = step(x)
    return x


def halves(x):
    high = x.astype(jnp.bfloat16)
    low = (x - high.astype(F32)).astype(jnp.bfloat16)
    return high, low


def product(a_high, a_low, b_high, b_low):
    dot = functools.partial(jnp.dot, preferred_element_type=F32)
    return dot(a_high, b_high) + (dot(a_high, b_low) + dot(a_low, b_high))


def accumulate(sector, count, target, left, right, field_high, field_low, outs):
    slot = pl.program_id(0)

    @pl.when(slot == 0)
    def _():
        for out in outs:
            out[...] = jnp.zeros_like(out)

    peers, rows, width = outs[0].shape

    @pl.when(slot < count[0, 0])
    def _():
        left_high, left_low = halves(left[0])
        inner = product(left_high, left_low, field_high[...], field_low[...])
        inner_high, inner_low = halves(inner)
        right_high, right_low = halves(right[0])
        result = product(inner_high, inner_low, right_high, right_low)
        goal = target[0, slot]
        kept = goal == sector
        swapped_here = goal == (sector ^ 1)
        roles = (jnp.logical_not(kept | swapped_here), kept, swapped_here)
        result = result.reshape(peers, HALVES * rows, width)
        for i, role in enumerate(roles):

            @pl.when(role)
            def _(i=i):
                for half in range(HALVES):
                    outs[i * HALVES + half][...] += result[:, half * rows : (half + 1) * rows]


def first_kernel(count, target, left, right, field, *rest):
    *outs, f_high, f_low = rest

    @pl.when(pl.program_id(0) == 0)
    def _():
        f_high[...], f_low[...] = halves(field[...])

    accumulate(lax.axis_index(SECTOR), count, target, left, right, f_high, f_low, outs)


def coefficients(sums):
    cross, norm_sq = sums[0:1, 0:1], sums[1:2, 0:1]
    scaled_cross, scaled_norm = sums[2:3, 0:1], sums[3:4, 0:1]
    rayleigh = cross / norm_sq
    return rayleigh, (scaled_cross - rayleigh * scaled_norm) / norm_sq


def corrected(coefs, vector, scaling, image):
    rayleigh, share = coefs
    return scaling * (image - rayleigh * vector) - share * vector


def second_kernel(count, target, left, right, sums, field, scaling, image, *rest):
    *outs, f_high, f_low = rest
    peers, slab, width = field.shape

    @pl.when(pl.program_id(0) == 0)
    def _():
        coefs = coefficients(sums)
        for peer in range(peers):
            value = corrected(coefs, field[peer], scaling[peer], image[peer])
            f_high[peer], f_low[peer] = halves(value)

    flat = (peers * slab, width)
    f_high, f_low = f_high.reshape(flat), f_low.reshape(flat)
    accumulate(lax.axis_index(SECTOR), count, target, left, right, f_high, f_low, outs)


def partial_image(body, counts, targets, left_stack, right_stack, fields, split, scratch=None, streamed=False):
    slots, width, _ = right_stack.shape

    def operand(i, count):
        return (jnp.minimum(i, count[0, 0] - 1), 0, 0)

    in_vmem = pl.BlockSpec(memory_space=pltpu.VMEM)
    targets, left_stack, right_stack = (
        pltpu.with_memory_space_constraint(x, pltpu.HBM)
        for x in (targets, left_stack, right_stack)
    )
    block = (width, width)
    part = (split[0], split[1] // HALVES, width)
    parts = 3 * HALVES
    field_spec = out_spec = in_vmem
    kind = jax.ShapeDtypeStruct
    if streamed:
        fields = [pltpu.with_memory_space_constraint(x, pltpu.HBM) for x in fields]
        field_spec = pl.BlockSpec(block, lambda i, *_: (0, 0), pipeline_mode=pl.Buffered(1))
        kind = pltpu.HBM
        out_spec = pl.BlockSpec(part, lambda i, *_: (0, 0, 0), pipeline_mode=pl.Buffered(1))
    return pl.pallas_call(
        body,
        out_shape=[kind(part, F32)] * parts,
        grid_spec=pltpu.PrefetchScalarGridSpec(
            num_scalar_prefetch=1,
            grid=(slots,),
            in_specs=[
                pl.BlockSpec(targets.shape, lambda i, *_: (0, 0), memory_space=pltpu.SMEM),
                pl.BlockSpec((1, width, width), operand),
                pl.BlockSpec((1, width, width), operand),
                *[field_spec] * len(fields),
            ],
            out_specs=[out_spec] * parts,
            scratch_shapes=[pltpu.VMEM(scratch or block, jnp.bfloat16)] * 2,
        ),
        compiler_params=pltpu.CompilerParams(
            dimension_semantics=("arbitrary",), vmem_limit_bytes=KERNEL_VMEM
        ),
        cost_estimate=pl.CostEstimate(
            flops=slots * 12 * width**3, bytes_accessed=slots * 8 * width**2, transcendentals=0
        ),
    )(counts, targets, left_stack, right_stack, *fields)


def place(half, along, across, size):
    return along * size + across if half == 0 else across * size + along


def spread(half, pieces, kept, crossed, local, weights=()):
    peers, rows, width = kept.shape
    size = len(pieces)
    me = lax.axis_index(TERM[half])
    lines = slice(half * rows, (half + 1) * rows)
    cross = scaled_cross = jnp.zeros((rows, width), F32)
    for k, piece in enumerate(pieces):
        for across in range(size):
            peer = place(half, lax.rem(me + k, size), across, size)
            total = kept[peer] + (crossed[peer] + local[peer])
            piece[across * rows : (across + 1) * rows] = total
            if weights:
                field, scaling = weights
                weighted = field[peer, lines] * total
                cross += weighted
                scaled_cross += scaling[peer, lines] * weighted
    return cross, scaled_cross


def first_spread(half, kept, crossed, local, field, scaling, *rest):
    *pieces, tail = rest
    rows = kept.shape[1]
    cross, scaled_cross = spread(half, pieces, kept, crossed, local, (field, scaling))
    me, lines = lax.axis_index(TERM), slice(half * rows, (half + 1) * rows)
    own = field[me, lines]
    square = own * own
    line = lax.broadcasted_iota(jnp.int32, tail.shape, 0)
    tile = jnp.zeros(tail.shape, F32)
    for i, part in enumerate((cross, square, scaled_cross, scaling[me, lines] * square)):
        tile = jnp.where(line == i, jnp.sum(part, keepdims=True), tile)
    tail[...] = tile
    for piece in pieces:
        piece[len(pieces) * rows :] = tail[...]


def second_spread(half, kept, crossed, local, *pieces):
    spread(half, pieces, kept, crossed, local)


def relay(axis, rows, *refs):
    size = len(refs) // 2
    arrived, pieces = refs[:size], refs[size:]
    me = lax.axis_index(axis)

    def summed(where):
        return functools.reduce(lambda x, y: x + y, [ref[where] for ref in arrived])

    for k, piece in enumerate(pieces):
        start = pl.multiple_of(lax.rem(me + k, size) * rows, rows)
        piece[:rows] = summed(pl.ds(start, rows))
        if piece.shape[0] > rows:
            piece[rows:] = summed(pl.ds(size * rows, piece.shape[0] - rows))


def landed(refs):
    size = len(refs) // HALVES
    groups = [refs[h * size : (h + 1) * size] for h in range(HALVES)]
    return [functools.reduce(lambda x, y: x + y, [r[...] for r in g]) for g in groups]


def first_landing(*refs):
    *arrived, image, copies, sums = refs
    rows = image.shape[0] // HALVES
    totals = landed(arrived)
    for half, total in enumerate(totals):
        image[half * rows : (half + 1) * rows] = total[:rows]
    for peer in range(copies.shape[0]):
        copies[peer] = image[...]
    sums[...] = functools.reduce(lambda x, y: x + y, totals)[rows:, : sums.shape[1]]


def second_landing(*refs):
    *arrived, sums, first_image, scaling, own, correction, image = refs
    rows = image.shape[0] // HALVES
    coefs = coefficients(sums)
    correction[...] = corrected(coefs, own[...], scaling[...], first_image[...])
    for half, total in enumerate(landed(arrived)):
        image[half * rows : (half + 1) * rows] = total


def repeated(x, copies):
    for peer in range(copies.shape[0]):
        copies[peer] = x[...]


def relayed(half, pieces, rows):
    arrived = exchanged_along(pieces, TERM[half])
    other = TERM[1 - half]
    shape = (rows + pieces[0].shape[0] - len(pieces) * rows, pieces[0].shape[1])
    onward = small_call(
        functools.partial(relay, other, rows), [shape] * len(pieces), arrived
    )
    return exchanged_along(onward, other)


def small_call(body, out_shapes, args, scratch=(), spaces=None):
    spaces = spaces or [pltpu.VMEM] * len(out_shapes)
    return pl.pallas_call(
        body,
        in_specs=[pl.BlockSpec(memory_space=pltpu.VMEM)] * len(args),
        out_specs=[
            pl.BlockSpec() if space == pltpu.HBM else pl.BlockSpec(memory_space=space)
            for space in spaces
        ],
        out_shape=[
            pltpu.HBM(s, F32) if space == pltpu.HBM else jax.ShapeDtypeStruct(s, F32)
            for s, space in zip(out_shapes, spaces)
        ],
        scratch_shapes=scratch,
        compiler_params=pltpu.CompilerParams(vmem_limit_bytes=SMALL_VMEM),
    )(*args)


def per_device(wavefunction, precond, left_ops, right_ops, out_sector, live_counts):
    peers = lax.axis_size(TERM)
    width = wavefunction.shape[1]
    slab = width // peers
    split = (peers, slab, width)
    rows = slab // HALVES
    size = lax.axis_size(TERM[0])
    field = wavefunction[0]
    blocked = field.reshape(split)
    scaling = precond[0]
    image_of = functools.partial(
        partial_image,
        counts=live_counts,
        targets=out_sector,
        left_stack=left_ops[0],
        right_stack=right_ops[0],
        split=split,
    )

    def moved_parts(parts):
        crossing, kept, local = (parts[i * HALVES : (i + 1) * HALVES] for i in range(3))
        return [(k, *moved(c, l)) for c, k, l in zip(crossing, kept, local)]

    (copies,) = small_call(repeated, [split], [scaling], spaces=[pltpu.HBM])
    full_scaling = swapped(copies)
    parts = image_of(first_kernel, fields=(field,), streamed=True)
    parts, full_scaling = lax.optimization_barrier((parts, full_scaling))
    parts = moved_parts(parts)
    arrived = []
    for half in range(HALVES):
        pieces = small_call(
            functools.partial(first_spread, half),
            [(size * rows + EXTRA, width)] * size,
            [*parts[half], blocked, full_scaling],
            [pltpu.VMEM((EXTRA, width), F32)],
        )
        arrived += relayed(half, pieces, rows)
    first_image, copies, sums = small_call(
        first_landing,
        [(slab, width), split, (EXTRA, LANES)],
        arrived,
        spaces=[pltpu.VMEM, pltpu.HBM, pltpu.VMEM],
    )
    full_image = swapped(copies)
    sums = over_sectors(sums)

    fields = (sums, blocked, full_scaling, full_image)
    parts = moved_parts(image_of(second_kernel, fields=fields, scratch=split))
    arrived = []
    for half in range(HALVES):
        pieces = small_call(
            functools.partial(second_spread, half), [(size * rows, width)] * size, parts[half]
        )
        arrived += relayed(half, pieces, rows)
    own = lax.dynamic_index_in_dim(blocked, lax.axis_index(TERM), 0, keepdims=False)
    correction, second_image = small_call(
        second_landing,
        [(slab, width)] * 2,
        [*arrived, sums, first_image, scaling, own],
    )
    return (first_image[None], correction[None], second_image[None])


def solution(mesh):
    torus = Mesh(mesh.devices.reshape(4, 4, 8, 2), ("term_0", "term_1", "sector_0", "sector_1"))
    placed = (
        P(SECTOR, None, None),
        P(SECTOR, TERM, None),
        P(SECTOR, TERM, None, None),
        P(SECTOR, TERM, None, None),
        P(SECTOR, TERM),
        P(SECTOR, TERM),
    )
    return jax.shard_map(
        per_device,
        mesh=torus,
        in_specs=placed,
        out_specs=(P(SECTOR, TERM, None), P(SECTOR, TERM, None), P(SECTOR, TERM, None)),
        check_vma=False,
    )
```

```python
import functools

import jax
import jax.numpy as jnp
from jax import lax
from jax.experimental import pallas as pl
from jax.experimental.pallas import tpu as pltpu
from jax.sharding import Mesh
from jax.sharding import PartitionSpec as P

TERM = ("term_0", "term_1")
SECTOR = ("sector_0", "sector_1")
LANES = 128
EXTRA = 8
HALVES = 2
MIB = 1 << 20
KERNEL_VMEM = 18 * MIB
SMALL_VMEM = 8 * MIB
F32 = jnp.float32


def moved(crossing, local):
    count = lax.axis_size(SECTOR)
    upward = [(i, i + 1) for i in range(1, count - 1, 2)]
    downward = [(j, i) for i, j in upward]
    swap = [(i, i ^ 1) for i in range(count)]
    return lax.ppermute(crossing, SECTOR, upward + downward), lax.ppermute(local, SECTOR, swap)


def exchanged_along(pieces, axis):
    size = len(pieces)
    routes = [[(i, (i + k) % size) for i in range(size)] for k in range(size)]
    sent = [lax.ppermute(pieces[k], axis, routes[k]) for k in range(1, size)]
    return [pieces[0], *sent]


def swapped(x):
    return lax.all_to_all(x, TERM, 0, 0, tiled=True)


def sector_steps():
    for axis in SECTOR[::-1]:
        count = lax.axis_size(axis)
        mask = 1
        while mask < count:
            yield functools.partial(exchanged, axis=axis, mask=mask)
            mask *= 2


def exchanged(x, axis, mask):
    pairs = [(i, i ^ mask) for i in range(lax.axis_size(axis))]
    return x + lax.ppermute(x, axis, pairs)


def over_sectors(x):
    for step in sector_steps():
        x = step(x)
    return x


def halves(x):
    high = x.astype(jnp.bfloat16)
    low = (x - high.astype(F32)).astype(jnp.bfloat16)
    return high, low


def product(a_high, a_low, b_high, b_low):
    dot = functools.partial(jnp.dot, preferred_element_type=F32)
    return dot(a_high, b_high) + (dot(a_high, b_low) + dot(a_low, b_high))


def accumulate(sector, count, target, left, right, field_high, field_low, outs):
    slot = pl.program_id(0)

    @pl.when(slot == 0)
    def _():
        for out in outs:
            out[...] = jnp.zeros_like(out)

    peers, rows, width = outs[0].shape

    @pl.when(slot < count[0, 0])
    def _():
        left_high, left_low = halves(left[0])
        inner = product(left_high, left_low, field_high[...], field_low[...])
        inner_high, inner_low = halves(inner)
        right_high, right_low = halves(right[0])
        result = product(inner_high, inner_low, right_high, right_low)
        goal = target[0, slot]
        kept = goal == sector
        swapped_here = goal == (sector ^ 1)
        roles = (jnp.logical_not(kept | swapped_here), kept, swapped_here)
        cuts = len(outs) // len(roles)
        result = result.reshape(peers, cuts * rows, width)
        for i, role in enumerate(roles):

            @pl.when(role)
            def _(i=i):
                for cut in range(cuts):
                    outs[i * cuts + cut][...] += result[:, cut * rows : (cut + 1) * rows]


def first_kernel(count, target, left, right, field, *rest):
    *outs, f_high, f_low = rest

    @pl.when(pl.program_id(0) == 0)
    def _():
        f_high[...], f_low[...] = halves(field[...])

    accumulate(lax.axis_index(SECTOR), count, target, left, right, f_high, f_low, outs)


def coefficients(sums):
    cross, norm_sq = sums[0:1, 0:1], sums[1:2, 0:1]
    scaled_cross, scaled_norm = sums[2:3, 0:1], sums[3:4, 0:1]
    rayleigh = cross / norm_sq
    return rayleigh, (scaled_cross - rayleigh * scaled_norm) / norm_sq


def corrected(coefs, vector, scaling, image):
    rayleigh, share = coefs
    return scaling * (image - rayleigh * vector) - share * vector


def second_kernel(count, target, left, right, sums, field, scaling, image, *rest):
    *outs, f_high, f_low = rest
    peers, slab, width = field.shape

    @pl.when(pl.program_id(0) == 0)
    def _():
        coefs = coefficients(sums)
        for peer in range(peers):
            value = corrected(coefs, field[peer], scaling[peer], image[peer])
            f_high[peer], f_low[peer] = halves(value)

    flat = (peers * slab, width)
    f_high, f_low = f_high.reshape(flat), f_low.reshape(flat)
    accumulate(lax.axis_index(SECTOR), count, target, left, right, f_high, f_low, outs)


def partial_image(body, counts, targets, left_stack, right_stack, fields, split, cuts, scratch=None, streamed=False):
    slots, width, _ = right_stack.shape

    def operand(i, count):
        return (jnp.minimum(i, count[0, 0] - 1), 0, 0)

    in_vmem = pl.BlockSpec(memory_space=pltpu.VMEM)
    targets, left_stack, right_stack = (
        pltpu.with_memory_space_constraint(x, pltpu.HBM)
        for x in (targets, left_stack, right_stack)
    )
    block = (width, width)
    part = (split[0], split[1] // cuts, width)
    field_spec = in_vmem
    if streamed:
        fields = [pltpu.with_memory_space_constraint(x, pltpu.HBM) for x in fields]
        field_spec = pl.BlockSpec(block, lambda i, *_: (0, 0), pipeline_mode=pl.Buffered(1))
    return pl.pallas_call(
        body,
        out_shape=[jax.ShapeDtypeStruct(part, F32)] * (3 * cuts),
        grid_spec=pltpu.PrefetchScalarGridSpec(
            num_scalar_prefetch=1,
            grid=(slots,),
            in_specs=[
                pl.BlockSpec(targets.shape, lambda i, *_: (0, 0), memory_space=pltpu.SMEM),
                pl.BlockSpec((1, width, width), operand),
                pl.BlockSpec((1, width, width), operand),
                *[field_spec] * len(fields),
            ],
            out_specs=[in_vmem] * (3 * cuts),
            scratch_shapes=[pltpu.VMEM(scratch or block, jnp.bfloat16)] * 2,
        ),
        compiler_params=pltpu.CompilerParams(
            dimension_semantics=("arbitrary",), vmem_limit_bytes=KERNEL_VMEM
        ),
        cost_estimate=pl.CostEstimate(
            flops=slots * 12 * width**3, bytes_accessed=slots * 8 * width**2, transcendentals=0
        ),
    )(counts, targets, left_stack, right_stack, *fields)


def place(half, along, across, size):
    return along * size + across if half == 0 else across * size + along


def spread(half, kept, crossed, local, *pieces):
    rows = kept.shape[1]
    size = len(pieces)
    me = lax.axis_index(TERM[half])
    for k, piece in enumerate(pieces):
        for across in range(size):
            peer = place(half, lax.rem(me + k, size), across, size)
            total = kept[peer] + (crossed[peer] + local[peer])
            piece[across * rows : (across + 1) * rows] = total


def relay(axis, rows, *refs):
    size = len(refs) // 2
    arrived, pieces = refs[:size], refs[size:]
    me = lax.axis_index(axis)
    for k, piece in enumerate(pieces):
        lines = pl.ds(pl.multiple_of(lax.rem(me + k, size) * rows, rows), rows)
        piece[...] = functools.reduce(lambda x, y: x + y, [ref[lines] for ref in arrived])


def landed(refs):
    size = len(refs) // HALVES
    groups = [refs[h * size : (h + 1) * size] for h in range(HALVES)]
    return [functools.reduce(lambda x, y: x + y, [r[...] for r in g]) for g in groups]


def tiles(x, slab, width):
    return [(c * slab, slice(c * LANES, (c + 1) * LANES)) for c in range(width // LANES)]


def combine(kept, crossed, local, field, scaling, packed, tail):
    peers, slab, width = kept.shape
    where = tiles(kept, slab, width)
    cross = scaled_cross = jnp.zeros((slab, width), F32)
    for peer in range(peers):
        total = kept[peer] + (crossed[peer] + local[peer])
        for row, lanes in where:
            packed[peer, row : row + slab] = total[:, lanes]
        weighted = field[peer] * total
        cross += weighted
        scaled_cross += scaling[peer] * weighted
    me = lax.axis_index(TERM)
    own = field[me]
    square = own * own
    line = lax.broadcasted_iota(jnp.int32, tail.shape, 0)
    tile = jnp.zeros(tail.shape, F32)
    for i, part in enumerate((cross, square, scaled_cross, scaling[me] * square)):
        tile = jnp.where(line == i, jnp.sum(part, keepdims=True), tile)
    tail[...] = tile
    for peer in range(peers):
        packed[peer, len(where) * slab :] = tail[...]


def first_landing(arrived, image, copies, sums):
    slab, width = image.shape
    total = functools.reduce(lambda x, y: x + y, [arrived[i] for i in range(arrived.shape[0])])
    where = tiles(image, slab, width)
    for row, lanes in where:
        image[:, lanes] = total[row : row + slab]
    for peer in range(copies.shape[0]):
        copies[peer] = image[...]
    sums[...] = total[len(where) * slab :]


def second_landing(*refs):
    *arrived, sums, first_image, scaling, own, correction, image = refs
    rows = image.shape[0] // HALVES
    coefs = coefficients(sums)
    correction[...] = corrected(coefs, own[...], scaling[...], first_image[...])
    for half, total in enumerate(landed(arrived)):
        image[half * rows : (half + 1) * rows] = total


def relayed(half, pieces, rows):
    arrived = exchanged_along(pieces, TERM[half])
    other = TERM[1 - half]
    shape = (rows, pieces[0].shape[1])
    onward = small_call(
        functools.partial(relay, other, rows), [shape] * len(pieces), arrived
    )
    return exchanged_along(onward, other)


def small_call(body, out_shapes, args, scratch=(), spaces=None):
    spaces = spaces or [pltpu.VMEM] * len(out_shapes)
    return pl.pallas_call(
        body,
        in_specs=[pl.BlockSpec(memory_space=pltpu.VMEM)] * len(args),
        out_specs=[
            pl.BlockSpec() if space == pltpu.HBM else pl.BlockSpec(memory_space=space)
            for space in spaces
        ],
        out_shape=[
            pltpu.HBM(s, F32) if space == pltpu.HBM else jax.ShapeDtypeStruct(s, F32)
            for s, space in zip(out_shapes, spaces)
        ],
        scratch_shapes=scratch,
        compiler_params=pltpu.CompilerParams(vmem_limit_bytes=SMALL_VMEM),
    )(*args)


def per_device(wavefunction, precond, left_ops, right_ops, out_sector, live_counts):
    peers = lax.axis_size(TERM)
    width = wavefunction.shape[1]
    slab = width // peers
    split = (peers, slab, width)
    rows = slab // HALVES
    size = lax.axis_size(TERM[0])
    field = wavefunction[0]
    blocked = field.reshape(split)
    scaling = precond[0]
    image_of = functools.partial(
        partial_image,
        counts=live_counts,
        targets=out_sector,
        left_stack=left_ops[0],
        right_stack=right_ops[0],
        split=split,
    )

    crossing, kept, local = image_of(first_kernel, fields=(field,), cuts=1, streamed=True)
    crossed, local = moved(crossing, local)
    scaling_late, _ = lax.optimization_barrier((scaling, kept))
    full_scaling = swapped(jnp.broadcast_to(scaling_late[None], split))
    (packed,) = small_call(
        combine,
        [(peers, slab * (width // LANES) + EXTRA, LANES)],
        [kept, crossed, local, blocked, full_scaling],
        [pltpu.VMEM((EXTRA, LANES), F32)],
    )
    first_image, copies, sums = small_call(
        first_landing,
        [(slab, width), split, (EXTRA, LANES)],
        [swapped(packed)],
        spaces=[pltpu.VMEM, pltpu.HBM, pltpu.VMEM],
    )
    full_image = swapped(copies)
    sums = over_sectors(sums)

    fields = (sums, blocked, full_scaling, full_image)
    parts = image_of(second_kernel, fields=fields, cuts=HALVES, scratch=split)
    crossing, kept, local = (parts[i * HALVES : (i + 1) * HALVES] for i in range(3))
    moves = [moved(c, l) for c, l in zip(crossing, local)]
    arrived = []
    for half in range(HALVES):
        pieces = small_call(
            functools.partial(spread, half),
            [(size * rows, width)] * size,
            [kept[half], *moves[half]],
        )
        arrived += relayed(half, pieces, rows)
    own = lax.dynamic_index_in_dim(blocked, lax.axis_index(TERM), 0, keepdims=False)
    correction, second_image = small_call(
        second_landing,
        [(slab, width)] * 2,
        [*arrived, sums, first_image, scaling, own],
    )
    return (first_image[None], correction[None], second_image[None])


def solution(mesh):
    torus = Mesh(mesh.devices.reshape(4, 4, 8, 2), ("term_0", "term_1", "sector_0", "sector_1"))
    placed = (
        P(SECTOR, None, None),
        P(SECTOR, TERM, None),
        P(SECTOR, TERM, None, None),
        P(SECTOR, TERM, None, None),
        P(SECTOR, TERM),
        P(SECTOR, TERM),
    )
    return jax.shard_map(
        per_device,
        mesh=torus,
        in_specs=placed,
        out_specs=(P(SECTOR, TERM, None), P(SECTOR, TERM, None), P(SECTOR, TERM, None)),
        check_vma=False,
    )
```

```python
import functools

import jax
import jax.numpy as jnp
from jax import lax
from jax.experimental import pallas as pl
from jax.experimental.pallas import tpu as pltpu
from jax.sharding import Mesh
from jax.sharding import PartitionSpec as P

TERM = ("term_0", "term_1")
SECTOR = ("sector_0", "sector_1")
LANES = 128
EXTRA = 8
HALVES = 2
MIB = 1 << 20
KERNEL_VMEM = 22 * MIB
SMALL_VMEM = 8 * MIB
F32 = jnp.float32


def moved(crossing, local):
    count = lax.axis_size(SECTOR)
    upward = [(i, i + 1) for i in range(1, count - 1, 2)]
    downward = [(j, i) for i, j in upward]
    swap = [(i, i ^ 1) for i in range(count)]
    return lax.ppermute(crossing, SECTOR, upward + downward), lax.ppermute(local, SECTOR, swap)


def exchanged_along(pieces, axis):
    size = len(pieces)
    routes = [[(i, (i + k) % size) for i in range(size)] for k in range(size)]
    sent = [lax.ppermute(pieces[k], axis, routes[k]) for k in range(1, size)]
    return [pieces[0], *sent]


def swapped(x):
    return lax.all_to_all(x, TERM, 0, 0, tiled=True)


def sector_steps():
    for axis in SECTOR[::-1]:
        count = lax.axis_size(axis)
        mask = 1
        while mask < count:
            yield functools.partial(exchanged, axis=axis, mask=mask)
            mask *= 2


def exchanged(x, axis, mask):
    pairs = [(i, i ^ mask) for i in range(lax.axis_size(axis))]
    return x + lax.ppermute(x, axis, pairs)


def over_sectors(x):
    for step in sector_steps():
        x = step(x)
    return x


def halves(x):
    high = x.astype(jnp.bfloat16)
    low = (x - high.astype(F32)).astype(jnp.bfloat16)
    return high, low


def product(a_high, a_low, b_high, b_low):
    dot = functools.partial(jnp.dot, preferred_element_type=F32)
    return dot(a_high, b_high) + (dot(a_high, b_low) + dot(a_low, b_high))


def fetches(slot, stacks, held, landed):
    return [
        pltpu.make_async_copy(stack.at[slot], place.at[slot], landed.at[i, slot])
        for i, (stack, place) in enumerate(zip(stacks, held))
    ]


def begin(stacks, held, landed, outs):
    for fetch in fetches(0, stacks, held, landed):
        fetch.start()
    for out in outs:
        out[...] = jnp.zeros_like(out)


def accumulate(sector, count, target, stacks, held, landed, field_high, field_low, outs):
    slot = pl.program_id(0)
    peers, rows, width = outs[0].shape

    @pl.when(slot < count[0, 0])
    def _():
        for fetch in fetches(slot, stacks, held, landed):
            fetch.wait()
        for later in range(1, stacks[0].shape[0]):

            @pl.when((slot == 0) & (later < count[0, 0]))
            def _(later=later):
                for fetch in fetches(later, stacks, held, landed):
                    fetch.start()

        left, right = held
        left_high, left_low = halves(left[slot])
        inner = product(left_high, left_low, field_high[...], field_low[...])
        inner_high, inner_low = halves(inner)
        right_high, right_low = halves(right[slot])
        result = product(inner_high, inner_low, right_high, right_low)
        goal = target[0, slot]
        kept = goal == sector
        swapped_here = goal == (sector ^ 1)
        roles = (jnp.logical_not(kept | swapped_here), kept, swapped_here)
        cuts = len(outs) // len(roles)
        result = result.reshape(peers, cuts * rows, width)
        for i, role in enumerate(roles):

            @pl.when(role)
            def _(i=i):
                for cut in range(cuts):
                    outs[i * cuts + cut][...] += result[:, cut * rows : (cut + 1) * rows]


def first_kernel(count, target, left, right, field, *rest):
    *outs, f_high, f_low, held_left, held_right, landed, whole, arrived = rest
    stacks, held = (left, right), (held_left, held_right)

    @pl.when(pl.program_id(0) == 0)
    def _():
        fetch = pltpu.make_async_copy(field, whole, arrived)
        fetch.start()
        begin(stacks, held, landed, outs)
        fetch.wait()
        f_high[...], f_low[...] = halves(whole[...])

    sector = lax.axis_index(SECTOR)
    accumulate(sector, count, target, stacks, held, landed, f_high, f_low, outs)


def coefficients(sums):
    cross, norm_sq = sums[0:1, 0:1], sums[1:2, 0:1]
    scaled_cross, scaled_norm = sums[2:3, 0:1], sums[3:4, 0:1]
    rayleigh = cross / norm_sq
    return rayleigh, (scaled_cross - rayleigh * scaled_norm) / norm_sq


def corrected(coefs, vector, scaling, image):
    rayleigh, share = coefs
    return scaling * (image - rayleigh * vector) - share * vector


def second_kernel(count, target, left, right, sums, field, scaling, image, *rest):
    *outs, f_high, f_low, held_left, held_right, landed = rest
    stacks, held = (left, right), (held_left, held_right)
    peers, slab, width = field.shape

    @pl.when(pl.program_id(0) == 0)
    def _():
        begin(stacks, held, landed, outs)
        coefs = coefficients(sums)
        for peer in range(peers):
            value = corrected(coefs, field[peer], scaling[peer], image[peer])
            f_high[peer], f_low[peer] = halves(value)

    flat = (peers * slab, width)
    f_high, f_low = f_high.reshape(flat), f_low.reshape(flat)
    sector = lax.axis_index(SECTOR)
    accumulate(sector, count, target, stacks, held, landed, f_high, f_low, outs)


def partial_image(body, counts, targets, left_stack, right_stack, fields, cuts, split):
    slots, width, _ = right_stack.shape
    in_vmem = pl.BlockSpec(memory_space=pltpu.VMEM)
    in_hbm = pl.BlockSpec(memory_space=pltpu.HBM)
    streamed = body is first_kernel
    targets, left_stack, right_stack = (
        pltpu.with_memory_space_constraint(x, pltpu.HBM)
        for x in (targets, left_stack, right_stack)
    )
    block = (width, width)
    part = (split[0], split[1] // cuts, width)
    scratch = [
        *[pltpu.VMEM(block if streamed else split, jnp.bfloat16)] * 2,
        *[pltpu.VMEM((slots, *block), F32)] * 2,
        pltpu.SemaphoreType.DMA((2, slots)),
    ]
    if streamed:
        fields = [pltpu.with_memory_space_constraint(x, pltpu.HBM) for x in fields]
        scratch += [pltpu.VMEM(block, F32), pltpu.SemaphoreType.DMA]
    return pl.pallas_call(
        body,
        out_shape=[jax.ShapeDtypeStruct(part, F32)] * (3 * cuts),
        grid_spec=pltpu.PrefetchScalarGridSpec(
            num_scalar_prefetch=1,
            grid=(slots,),
            in_specs=[
                pl.BlockSpec(targets.shape, lambda i, *_: (0, 0), memory_space=pltpu.SMEM),
                in_hbm,
                in_hbm,
                *[in_hbm if streamed else in_vmem] * len(fields),
            ],
            out_specs=[in_vmem] * (3 * cuts),
            scratch_shapes=scratch,
        ),
        compiler_params=pltpu.CompilerParams(
            dimension_semantics=("arbitrary",), vmem_limit_bytes=KERNEL_VMEM
        ),
        cost_estimate=pl.CostEstimate(
            flops=slots * 12 * width**3, bytes_accessed=slots * 8 * width**2, transcendentals=0
        ),
    )(counts, targets, left_stack, right_stack, *fields)


def place(half, along, across, size):
    return along * size + across if half == 0 else across * size + along


def spread(half, kept, crossed, local, *pieces):
    rows = kept.shape[1]
    size = len(pieces)
    me = lax.axis_index(TERM[half])
    for k, piece in enumerate(pieces):
        for across in range(size):
            peer = place(half, lax.rem(me + k, size), across, size)
            total = kept[peer] + (crossed[peer] + local[peer])
            piece[across * rows : (across + 1) * rows] = total


def relay(axis, rows, *refs):
    size = len(refs) // 2
    arrived, pieces = refs[:size], refs[size:]
    me = lax.axis_index(axis)
    for k, piece in enumerate(pieces):
        lines = pl.ds(pl.multiple_of(lax.rem(me + k, size) * rows, rows), rows)
        piece[...] = functools.reduce(lambda x, y: x + y, [ref[lines] for ref in arrived])


def landed(refs):
    size = len(refs) // HALVES
    groups = [refs[h * size : (h + 1) * size] for h in range(HALVES)]
    return [functools.reduce(lambda x, y: x + y, [r[...] for r in g]) for g in groups]


def tiles(x, slab, width):
    return [(c * slab, slice(c * LANES, (c + 1) * LANES)) for c in range(width // LANES)]


def combine(kept, crossed, local, field, scaling, packed, tail):
    peers, slab, width = kept.shape
    where = tiles(kept, slab, width)
    cross = scaled_cross = jnp.zeros((slab, width), F32)
    for peer in range(peers):
        total = kept[peer] + (crossed[peer] + local[peer])
        for row, lanes in where:
            packed[peer, row : row + slab] = total[:, lanes]
        weighted = field[peer] * total
        cross += weighted
        scaled_cross += scaling[peer] * weighted
    me = lax.axis_index(TERM)
    own = field[me]
    square = own * own
    line = lax.broadcasted_iota(jnp.int32, tail.shape, 0)
    tile = jnp.zeros(tail.shape, F32)
    for i, part in enumerate((cross, square, scaled_cross, scaling[me] * square)):
        tile = jnp.where(line == i, jnp.sum(part, keepdims=True), tile)
    tail[...] = tile
    for peer in range(peers):
        packed[peer, len(where) * slab :] = tail[...]


def first_landing(arrived, image, copies, sums):
    slab, width = image.shape
    total = functools.reduce(lambda x, y: x + y, [arrived[i] for i in range(arrived.shape[0])])
    where = tiles(image, slab, width)
    for row, lanes in where:
        image[:, lanes] = total[row : row + slab]
    for peer in range(copies.shape[0]):
        copies[peer] = image[...]
    sums[...] = total[len(where) * slab :]


def second_landing(*refs):
    *arrived, sums, first_image, scaling, own, correction, image = refs
    rows = image.shape[0] // HALVES
    coefs = coefficients(sums)
    correction[...] = corrected(coefs, own[...], scaling[...], first_image[...])
    for half, total in enumerate(landed(arrived)):
        image[half * rows : (half + 1) * rows] = total


def relayed(half, pieces, rows):
    arrived = exchanged_along(pieces, TERM[half])
    other = TERM[1 - half]
    shape = (rows, pieces[0].shape[1])
    onward = small_call(
        functools.partial(relay, other, rows), [shape] * len(pieces), arrived
    )
    return exchanged_along(onward, other)


def small_call(body, out_shapes, args, scratch=(), spaces=None):
    spaces = spaces or [pltpu.VMEM] * len(out_shapes)
    return pl.pallas_call(
        body,
        in_specs=[pl.BlockSpec(memory_space=pltpu.VMEM)] * len(args),
        out_specs=[
            pl.BlockSpec() if space == pltpu.HBM else pl.BlockSpec(memory_space=space)
            for space in spaces
        ],
        out_shape=[
            pltpu.HBM(s, F32) if space == pltpu.HBM else jax.ShapeDtypeStruct(s, F32)
            for s, space in zip(out_shapes, spaces)
        ],
        scratch_shapes=scratch,
        compiler_params=pltpu.CompilerParams(vmem_limit_bytes=SMALL_VMEM),
    )(*args)


def per_device(wavefunction, precond, left_ops, right_ops, out_sector, live_counts):
    peers = lax.axis_size(TERM)
    width = wavefunction.shape[1]
    slab = width // peers
    split = (peers, slab, width)
    rows = slab // HALVES
    size = lax.axis_size(TERM[0])
    field = wavefunction[0]
    blocked = field.reshape(split)
    scaling = precond[0]
    image_of = functools.partial(
        partial_image,
        counts=live_counts,
        targets=out_sector,
        left_stack=left_ops[0],
        right_stack=right_ops[0],
        split=split,
    )

    crossing, kept, local = image_of(first_kernel, fields=(field,), cuts=1)
    crossed, local = moved(crossing, local)
    scaling_late, _ = lax.optimization_barrier((scaling, kept))
    full_scaling = swapped(jnp.broadcast_to(scaling_late[None], split))
    (packed,) = small_call(
        combine,
        [(peers, slab * (width // LANES) + EXTRA, LANES)],
        [kept, crossed, local, blocked, full_scaling],
        [pltpu.VMEM((EXTRA, LANES), F32)],
    )
    first_image, copies, sums = small_call(
        first_landing,
        [(slab, width), split, (EXTRA, LANES)],
        [swapped(packed)],
        spaces=[pltpu.VMEM, pltpu.HBM, pltpu.VMEM],
    )
    full_image = swapped(copies)
    sums = over_sectors(sums)

    fields = (sums, blocked, full_scaling, full_image)
    parts = image_of(second_kernel, fields=fields, cuts=HALVES)
    crossing, kept, local = (parts[i * HALVES : (i + 1) * HALVES] for i in range(3))
    moves = [moved(c, l) for c, l in zip(crossing, local)]
    arrived = []
    for half in range(HALVES):
        pieces = small_call(
            functools.partial(spread, half),
            [(size * rows, width)] * size,
            [kept[half], *moves[half]],
        )
        arrived += relayed(half, pieces, rows)
    own = lax.dynamic_index_in_dim(blocked, lax.axis_index(TERM), 0, keepdims=False)
    correction, second_image = small_call(
        second_landing,
        [(slab, width)] * 2,
        [*arrived, sums, first_image, scaling, own],
    )
    return (first_image[None], correction[None], second_image[None])


def solution(mesh):
    torus = Mesh(mesh.devices.reshape(4, 4, 8, 2), ("term_0", "term_1", "sector_0", "sector_1"))
    placed = (
        P(SECTOR, None, None),
        P(SECTOR, TERM, None),
        P(SECTOR, TERM, None, None),
        P(SECTOR, TERM, None, None),
        P(SECTOR, TERM),
        P(SECTOR, TERM),
    )
    return jax.shard_map(
        per_device,
        mesh=torus,
        in_specs=placed,
        out_specs=(P(SECTOR, TERM, None), P(SECTOR, TERM, None), P(SECTOR, TERM, None)),
        check_vma=False,
    )
```

```python
import functools

import jax
import jax.numpy as jnp
from jax import lax
from jax.experimental import pallas as pl
from jax.experimental.pallas import tpu as pltpu
from jax.sharding import Mesh
from jax.sharding import PartitionSpec as P

TERM = ("term_0", "term_1")
SECTOR = ("sector_0", "sector_1")
LANES = 128
EXTRA = 8
HALVES = 2
MIB = 1 << 20
KERNEL_VMEM = 22 * MIB
SMALL_VMEM = 8 * MIB
F32 = jnp.float32


def moved(crossing, local):
    count = lax.axis_size(SECTOR)
    upward = [(i, i + 1) for i in range(1, count - 1, 2)]
    downward = [(j, i) for i, j in upward]
    swap = [(i, i ^ 1) for i in range(count)]
    return lax.ppermute(crossing, SECTOR, upward + downward), lax.ppermute(local, SECTOR, swap)


def exchanged_along(pieces, axis):
    size = len(pieces)
    routes = [[(i, (i + k) % size) for i in range(size)] for k in range(size)]
    sent = [lax.ppermute(pieces[k], axis, routes[k]) for k in range(1, size)]
    return [pieces[0], *sent]


def swapped(x):
    return lax.all_to_all(x, TERM, 0, 0, tiled=True)


def sector_steps():
    for axis in SECTOR[::-1]:
        count = lax.axis_size(axis)
        mask = 1
        while mask < count:
            yield functools.partial(exchanged, axis=axis, mask=mask)
            mask *= 2


def exchanged(x, axis, mask):
    pairs = [(i, i ^ mask) for i in range(lax.axis_size(axis))]
    return x + lax.ppermute(x, axis, pairs)


def over_sectors(x):
    for step in sector_steps():
        x = step(x)
    return x


def halves(x):
    high = x.astype(jnp.bfloat16)
    low = (x - high.astype(F32)).astype(jnp.bfloat16)
    return high, low


def product(a_high, a_low, b_high, b_low):
    dot = functools.partial(jnp.dot, preferred_element_type=F32)
    return dot(a_high, b_high) + (dot(a_high, b_low) + dot(a_low, b_high))


def fetches(slot, stacks, held, landed):
    return [
        pltpu.make_async_copy(stack.at[slot], place.at[slot], landed.at[i, slot])
        for i, (stack, place) in enumerate(zip(stacks, held))
    ]


def begin(stacks, held, landed, outs):
    for fetch in fetches(0, stacks, held, landed):
        fetch.start()
    for out in outs:
        out[...] = jnp.zeros_like(out)


def accumulate(sector, count, target, stacks, held, landed, field_high, field_low, outs):
    slot = pl.program_id(0)
    peers, rows, width = outs[0].shape

    @pl.when(slot < count[0, 0])
    def _():
        for fetch in fetches(slot, stacks, held, landed):
            fetch.wait()
        for later in range(1, stacks[0].shape[0]):

            @pl.when((slot == 0) & (later < count[0, 0]))
            def _(later=later):
                for fetch in fetches(later, stacks, held, landed):
                    fetch.start()

        left, right = held
        left_high, left_low = halves(left[slot])
        inner = product(left_high, left_low, field_high[...], field_low[...])
        inner_high, inner_low = halves(inner)
        right_high, right_low = halves(right[slot])
        result = product(inner_high, inner_low, right_high, right_low)
        goal = target[0, slot]
        kept = goal == sector
        swapped_here = goal == (sector ^ 1)
        roles = (jnp.logical_not(kept | swapped_here), kept, swapped_here)
        cuts = len(outs) // len(roles)
        result = result.reshape(peers, cuts * rows, width)
        for i, role in enumerate(roles):

            @pl.when(role)
            def _(i=i):
                for cut in range(cuts):
                    outs[i * cuts + cut][...] += result[:, cut * rows : (cut + 1) * rows]


def first_kernel(count, target, left, right, field, *rest):
    *outs, f_high, f_low, held_left, held_right, landed, whole, arrived = rest
    stacks, held = (left, right), (held_left, held_right)

    @pl.when(pl.program_id(0) == 0)
    def _():
        fetch = pltpu.make_async_copy(field, whole, arrived)
        fetch.start()
        begin(stacks, held, landed, outs)
        fetch.wait()
        f_high[...], f_low[...] = halves(whole[...])

    sector = lax.axis_index(SECTOR)
    accumulate(sector, count, target, stacks, held, landed, f_high, f_low, outs)


def coefficients(sums):
    cross, norm_sq = sums[0:1, 0:1], sums[1:2, 0:1]
    scaled_cross, scaled_norm = sums[2:3, 0:1], sums[3:4, 0:1]
    rayleigh = cross / norm_sq
    return rayleigh, (scaled_cross - rayleigh * scaled_norm) / norm_sq


def corrected(coefs, vector, scaling, image):
    rayleigh, share = coefs
    return scaling * (image - rayleigh * vector) - share * vector


def second_kernel(count, target, left, right, sums, field, scaling, image, *rest):
    *outs, f_high, f_low, held_left, held_right, landed = rest
    stacks, held = (left, right), (held_left, held_right)
    peers, slab, width = field.shape

    @pl.when(pl.program_id(0) == 0)
    def _():
        begin(stacks, held, landed, outs)
        coefs = coefficients(sums)
        for peer in range(peers):
            value = corrected(coefs, field[peer], scaling[peer], image[peer])
            f_high[peer], f_low[peer] = halves(value)

    flat = (peers * slab, width)
    f_high, f_low = f_high.reshape(flat), f_low.reshape(flat)
    sector = lax.axis_index(SECTOR)
    accumulate(sector, count, target, stacks, held, landed, f_high, f_low, outs)


def partial_image(body, counts, targets, left_stack, right_stack, fields, cuts, split):
    slots, width, _ = right_stack.shape
    in_vmem = pl.BlockSpec(memory_space=pltpu.VMEM)
    in_hbm = pl.BlockSpec(memory_space=pltpu.HBM)
    streamed = body is first_kernel
    targets, left_stack, right_stack = (
        pltpu.with_memory_space_constraint(x, pltpu.HBM)
        for x in (targets, left_stack, right_stack)
    )
    block = (width, width)
    part = (split[0], split[1] // cuts, width)
    scratch = [
        *[pltpu.VMEM(block if streamed else split, jnp.bfloat16)] * 2,
        *[pltpu.VMEM((slots, *block), F32)] * 2,
        pltpu.SemaphoreType.DMA((2, slots)),
    ]
    if streamed:
        fields = [pltpu.with_memory_space_constraint(x, pltpu.HBM) for x in fields]
        scratch += [pltpu.VMEM(block, F32), pltpu.SemaphoreType.DMA]
    return pl.pallas_call(
        body,
        out_shape=[jax.ShapeDtypeStruct(part, F32)] * (3 * cuts),
        grid_spec=pltpu.PrefetchScalarGridSpec(
            num_scalar_prefetch=1,
            grid=(slots,),
            in_specs=[
                pl.BlockSpec(targets.shape, lambda i, *_: (0, 0), memory_space=pltpu.SMEM),
                in_hbm,
                in_hbm,
                *[in_hbm if streamed else in_vmem] * len(fields),
            ],
            out_specs=[in_vmem] * (3 * cuts),
            scratch_shapes=scratch,
        ),
        compiler_params=pltpu.CompilerParams(
            dimension_semantics=("arbitrary",), vmem_limit_bytes=KERNEL_VMEM
        ),
        cost_estimate=pl.CostEstimate(
            flops=slots * 12 * width**3, bytes_accessed=slots * 8 * width**2, transcendentals=0
        ),
    )(counts, targets, left_stack, right_stack, *fields)


def spread(kept, crossed, local, *pieces):
    rows = kept.shape[1]
    size = len(pieces)
    me = lax.axis_index(TERM[0])
    for k, piece in enumerate(pieces):
        first = lax.rem(me + k, size) * size
        for across in range(size):
            peer = first + across
            total = kept[peer] + (crossed[peer] + local[peer])
            piece[across * rows : (across + 1) * rows] = total


def summed(refs, lines):
    return functools.reduce(lambda x, y: x + y, [ref[lines] for ref in refs])


def relay(*refs):
    size = len(refs) // (HALVES + 1)
    arrived, pieces = refs[: HALVES * size], refs[HALVES * size :]
    rows = pieces[0].shape[0] // HALVES
    me = lax.axis_index(TERM[1])
    for k, piece in enumerate(pieces):
        lines = pl.ds(pl.multiple_of(lax.rem(me + k, size) * rows, rows), rows)
        for half in range(HALVES):
            group = arrived[half * size : (half + 1) * size]
            piece[half * rows : (half + 1) * rows] = summed(group, lines)


def tiles(x, slab, width):
    return [(c * slab, slice(c * LANES, (c + 1) * LANES)) for c in range(width // LANES)]


def combine(kept, crossed, local, field, scaling, packed, tail):
    peers, slab, width = kept.shape
    where = tiles(kept, slab, width)
    cross = scaled_cross = jnp.zeros((slab, width), F32)
    for peer in range(peers):
        total = kept[peer] + (crossed[peer] + local[peer])
        for row, lanes in where:
            packed[peer, row : row + slab] = total[:, lanes]
        weighted = field[peer] * total
        cross += weighted
        scaled_cross += scaling[peer] * weighted
    me = lax.axis_index(TERM)
    own = field[me]
    square = own * own
    line = lax.broadcasted_iota(jnp.int32, tail.shape, 0)
    tile = jnp.zeros(tail.shape, F32)
    for i, part in enumerate((cross, square, scaled_cross, scaling[me] * square)):
        tile = jnp.where(line == i, jnp.sum(part, keepdims=True), tile)
    tail[...] = tile
    for peer in range(peers):
        packed[peer, len(where) * slab :] = tail[...]


def first_landing(arrived, image, copies, sums):
    slab, width = image.shape
    total = functools.reduce(lambda x, y: x + y, [arrived[i] for i in range(arrived.shape[0])])
    where = tiles(image, slab, width)
    for row, lanes in where:
        image[:, lanes] = total[row : row + slab]
    for peer in range(copies.shape[0]):
        copies[peer] = image[...]
    sums[...] = total[len(where) * slab :]


def second_landing(*refs):
    *arrived, sums, first_image, scaling, own, correction, image = refs
    coefs = coefficients(sums)
    correction[...] = corrected(coefs, own[...], scaling[...], first_image[...])
    image[...] = summed(arrived, ...)


def small_call(body, out_shapes, args, scratch=(), spaces=None):
    spaces = spaces or [pltpu.VMEM] * len(out_shapes)
    return pl.pallas_call(
        body,
        in_specs=[pl.BlockSpec(memory_space=pltpu.VMEM)] * len(args),
        out_specs=[
            pl.BlockSpec() if space == pltpu.HBM else pl.BlockSpec(memory_space=space)
            for space in spaces
        ],
        out_shape=[
            pltpu.HBM(s, F32) if space == pltpu.HBM else jax.ShapeDtypeStruct(s, F32)
            for s, space in zip(out_shapes, spaces)
        ],
        scratch_shapes=scratch,
        compiler_params=pltpu.CompilerParams(vmem_limit_bytes=SMALL_VMEM),
    )(*args)


def per_device(wavefunction, precond, left_ops, right_ops, out_sector, live_counts):
    peers = lax.axis_size(TERM)
    width = wavefunction.shape[1]
    slab = width // peers
    split = (peers, slab, width)
    rows = slab // HALVES
    size = lax.axis_size(TERM[0])
    field = wavefunction[0]
    blocked = field.reshape(split)
    scaling = precond[0]
    image_of = functools.partial(
        partial_image,
        counts=live_counts,
        targets=out_sector,
        left_stack=left_ops[0],
        right_stack=right_ops[0],
        split=split,
    )

    crossing, kept, local = image_of(first_kernel, fields=(field,), cuts=1)
    crossed, local = moved(crossing, local)
    scaling_late, _ = lax.optimization_barrier((scaling, kept))
    full_scaling = swapped(jnp.broadcast_to(scaling_late[None], split))
    (packed,) = small_call(
        combine,
        [(peers, slab * (width // LANES) + EXTRA, LANES)],
        [kept, crossed, local, blocked, full_scaling],
        [pltpu.VMEM((EXTRA, LANES), F32)],
    )
    first_image, copies, sums = small_call(
        first_landing,
        [(slab, width), split, (EXTRA, LANES)],
        [swapped(packed)],
        spaces=[pltpu.VMEM, pltpu.HBM, pltpu.VMEM],
    )
    full_image = swapped(copies)
    sums = over_sectors(sums)

    fields = (sums, blocked, full_scaling, full_image)
    parts = image_of(second_kernel, fields=fields, cuts=HALVES)
    crossing, kept, local = (parts[i * HALVES : (i + 1) * HALVES] for i in range(3))
    moves = [moved(c, l) for c, l in zip(crossing, local)]
    arrived = []
    for half in range(HALVES):
        pieces = small_call(
            spread, [(size * rows, width)] * size, [kept[half], *moves[half]]
        )
        arrived += exchanged_along(pieces, TERM[0])
    pieces = small_call(relay, [(slab, width)] * size, arrived)
    arrived = exchanged_along(pieces, TERM[1])
    own = lax.dynamic_index_in_dim(blocked, lax.axis_index(TERM), 0, keepdims=False)
    correction, second_image = small_call(
        second_landing,
        [(slab, width)] * 2,
        [*arrived, sums, first_image, scaling, own],
    )
    return (first_image[None], correction[None], second_image[None])


def solution(mesh):
    torus = Mesh(mesh.devices.reshape(4, 4, 8, 2), ("term_0", "term_1", "sector_0", "sector_1"))
    placed = (
        P(SECTOR, None, None),
        P(SECTOR, TERM, None),
        P(SECTOR, TERM, None, None),
        P(SECTOR, TERM, None, None),
        P(SECTOR, TERM),
        P(SECTOR, TERM),
    )
    return jax.shard_map(
        per_device,
        mesh=torus,
        in_specs=placed,
        out_specs=(P(SECTOR, TERM, None), P(SECTOR, TERM, None), P(SECTOR, TERM, None)),
        check_vma=False,
    )
```

```python
import functools

import jax
import jax.numpy as jnp
from jax import lax
from jax.experimental import pallas as pl
from jax.experimental.pallas import tpu as pltpu
from jax.sharding import Mesh
from jax.sharding import PartitionSpec as P

TERM = ("term_0", "term_1")
SECTOR = ("sector_0", "sector_1")
LANES = 128
EXTRA = 8
SHARES = (3, 1)
MIB = 1 << 20
KERNEL_VMEM = 22 * MIB
SMALL_VMEM = 8 * MIB
F32 = jnp.float32


def moved(crossing, local):
    count = lax.axis_size(SECTOR)
    upward = [(i, i + 1) for i in range(1, count - 1, 2)]
    downward = [(j, i) for i, j in upward]
    swap = [(i, i ^ 1) for i in range(count)]
    return lax.ppermute(crossing, SECTOR, upward + downward), lax.ppermute(local, SECTOR, swap)


def exchanged_along(pieces, axis):
    size = len(pieces)
    routes = [[(i, (i + k) % size) for i in range(size)] for k in range(size)]
    sent = [lax.ppermute(pieces[k], axis, routes[k]) for k in range(1, size)]
    return [pieces[0], *sent]


def swapped(x):
    return lax.all_to_all(x, TERM, 0, 0, tiled=True)


def sector_steps():
    for axis in SECTOR[::-1]:
        count = lax.axis_size(axis)
        mask = 1
        while mask < count:
            yield functools.partial(exchanged, axis=axis, mask=mask)
            mask *= 2


def exchanged(x, axis, mask):
    pairs = [(i, i ^ mask) for i in range(lax.axis_size(axis))]
    return x + lax.ppermute(x, axis, pairs)


def over_sectors(x):
    for step in sector_steps():
        x = step(x)
    return x


def halves(x):
    high = x.astype(jnp.bfloat16)
    low = (x - high.astype(F32)).astype(jnp.bfloat16)
    return high, low


def product(a_high, a_low, b_high, b_low):
    dot = functools.partial(jnp.dot, preferred_element_type=F32)
    return dot(a_high, b_high) + (dot(a_high, b_low) + dot(a_low, b_high))


def fetches(slot, stacks, held, landed):
    return [
        pltpu.make_async_copy(stack.at[slot], place.at[slot], landed.at[i, slot])
        for i, (stack, place) in enumerate(zip(stacks, held))
    ]


def begin(stacks, held, landed, outs):
    for fetch in fetches(0, stacks, held, landed):
        fetch.start()
    for out in outs:
        out[...] = jnp.zeros_like(out)


def accumulate(sector, count, target, stacks, held, landed, field_high, field_low, outs):
    slot = pl.program_id(0)
    peers, _, width = outs[0].shape

    @pl.when(slot < count[0, 0])
    def _():
        for fetch in fetches(slot, stacks, held, landed):
            fetch.wait()
        for later in range(1, stacks[0].shape[0]):

            @pl.when((slot == 0) & (later < count[0, 0]))
            def _(later=later):
                for fetch in fetches(later, stacks, held, landed):
                    fetch.start()

        left, right = held
        left_high, left_low = halves(left[slot])
        inner = product(left_high, left_low, field_high[...], field_low[...])
        inner_high, inner_low = halves(inner)
        right_high, right_low = halves(right[slot])
        result = product(inner_high, inner_low, right_high, right_low)
        goal = target[0, slot]
        kept = goal == sector
        swapped_here = goal == (sector ^ 1)
        roles = (jnp.logical_not(kept | swapped_here), kept, swapped_here)
        cuts = len(outs) // len(roles)
        rows = [out.shape[1] for out in outs[:cuts]]
        ends = [sum(rows[: i + 1]) for i in range(cuts)]
        result = result.reshape(peers, ends[-1], width)
        for i, role in enumerate(roles):

            @pl.when(role)
            def _(i=i):
                for cut in range(cuts):
                    outs[i * cuts + cut][...] += result[:, ends[cut] - rows[cut] : ends[cut]]


def first_kernel(count, target, left, right, field, *rest):
    *outs, f_high, f_low, held_left, held_right, landed, whole, arrived = rest
    stacks, held = (left, right), (held_left, held_right)

    @pl.when(pl.program_id(0) == 0)
    def _():
        fetch = pltpu.make_async_copy(field, whole, arrived)
        fetch.start()
        begin(stacks, held, landed, outs)
        fetch.wait()
        f_high[...], f_low[...] = halves(whole[...])

    sector = lax.axis_index(SECTOR)
    accumulate(sector, count, target, stacks, held, landed, f_high, f_low, outs)


def coefficients(sums):
    cross, norm_sq = sums[0:1, 0:1], sums[1:2, 0:1]
    scaled_cross, scaled_norm = sums[2:3, 0:1], sums[3:4, 0:1]
    rayleigh = cross / norm_sq
    return rayleigh, (scaled_cross - rayleigh * scaled_norm) / norm_sq


def corrected(coefs, vector, scaling, image):
    rayleigh, share = coefs
    return scaling * (image - rayleigh * vector) - share * vector


def second_kernel(count, target, left, right, sums, field, scaling, image, *rest):
    *outs, f_high, f_low, held_left, held_right, landed = rest
    stacks, held = (left, right), (held_left, held_right)
    peers, slab, width = field.shape

    @pl.when(pl.program_id(0) == 0)
    def _():
        begin(stacks, held, landed, outs)
        coefs = coefficients(sums)
        for peer in range(peers):
            value = corrected(coefs, field[peer], scaling[peer], image[peer])
            f_high[peer], f_low[peer] = halves(value)

    flat = (peers * slab, width)
    f_high, f_low = f_high.reshape(flat), f_low.reshape(flat)
    sector = lax.axis_index(SECTOR)
    accumulate(sector, count, target, stacks, held, landed, f_high, f_low, outs)


def partial_image(body, counts, targets, left_stack, right_stack, fields, cuts, split):
    slots, width, _ = right_stack.shape
    in_vmem = pl.BlockSpec(memory_space=pltpu.VMEM)
    in_hbm = pl.BlockSpec(memory_space=pltpu.HBM)
    streamed = body is first_kernel
    targets, left_stack, right_stack = (
        pltpu.with_memory_space_constraint(x, pltpu.HBM)
        for x in (targets, left_stack, right_stack)
    )
    block = (width, width)
    parts = [(split[0], rows, width) for rows in cuts] * 3
    scratch = [
        *[pltpu.VMEM(block if streamed else split, jnp.bfloat16)] * 2,
        *[pltpu.VMEM((slots, *block), F32)] * 2,
        pltpu.SemaphoreType.DMA((2, slots)),
    ]
    if streamed:
        fields = [pltpu.with_memory_space_constraint(x, pltpu.HBM) for x in fields]
        scratch += [pltpu.VMEM(block, F32), pltpu.SemaphoreType.DMA]
    return pl.pallas_call(
        body,
        out_shape=[jax.ShapeDtypeStruct(part, F32) for part in parts],
        grid_spec=pltpu.PrefetchScalarGridSpec(
            num_scalar_prefetch=1,
            grid=(slots,),
            in_specs=[
                pl.BlockSpec(targets.shape, lambda i, *_: (0, 0), memory_space=pltpu.SMEM),
                in_hbm,
                in_hbm,
                *[in_hbm if streamed else in_vmem] * len(fields),
            ],
            out_specs=[in_vmem] * len(parts),
            scratch_shapes=scratch,
        ),
        compiler_params=pltpu.CompilerParams(
            dimension_semantics=("arbitrary",), vmem_limit_bytes=KERNEL_VMEM
        ),
        cost_estimate=pl.CostEstimate(
            flops=slots * 12 * width**3, bytes_accessed=slots * 8 * width**2, transcendentals=0
        ),
    )(counts, targets, left_stack, right_stack, *fields)


def spread(kept, crossed, local, *pieces):
    rows = kept.shape[1]
    size = len(pieces)
    me = lax.axis_index(TERM[0])
    for k, piece in enumerate(pieces):
        first = lax.rem(me + k, size) * size
        for across in range(size):
            peer = first + across
            total = kept[peer] + (crossed[peer] + local[peer])
            piece[across * rows : (across + 1) * rows] = total


def summed(refs, lines):
    return functools.reduce(lambda x, y: x + y, [ref[lines] for ref in refs])


def relay(*refs):
    size = len(refs) // (len(SHARES) + 1)
    arrived, pieces = refs[: len(SHARES) * size], refs[len(SHARES) * size :]
    me = lax.axis_index(TERM[1])
    for k, piece in enumerate(pieces):
        end = 0
        for part in range(len(SHARES)):
            group = arrived[part * size : (part + 1) * size]
            rows = group[0].shape[0] // size
            lines = pl.ds(pl.multiple_of(lax.rem(me + k, size) * rows, rows), rows)
            piece[end : end + rows] = summed(group, lines)
            end += rows


def tiles(x, slab, width):
    return [(c * slab, slice(c * LANES, (c + 1) * LANES)) for c in range(width // LANES)]


def combine(kept, crossed, local, field, scaling, packed, tail):
    peers, slab, width = kept.shape
    where = tiles(kept, slab, width)
    cross = scaled_cross = jnp.zeros((slab, width), F32)
    for peer in range(peers):
        total = kept[peer] + (crossed[peer] + local[peer])
        for row, lanes in where:
            packed[peer, row : row + slab] = total[:, lanes]
        weighted = field[peer] * total
        cross += weighted
        scaled_cross += scaling[peer] * weighted
    me = lax.axis_index(TERM)
    own = field[me]
    square = own * own
    line = lax.broadcasted_iota(jnp.int32, tail.shape, 0)
    tile = jnp.zeros(tail.shape, F32)
    for i, part in enumerate((cross, square, scaled_cross, scaling[me] * square)):
        tile = jnp.where(line == i, jnp.sum(part, keepdims=True), tile)
    tail[...] = tile
    for peer in range(peers):
        packed[peer, len(where) * slab :] = tail[...]


def first_landing(arrived, image, copies, sums):
    slab, width = image.shape
    total = functools.reduce(lambda x, y: x + y, [arrived[i] for i in range(arrived.shape[0])])
    where = tiles(image, slab, width)
    for row, lanes in where:
        image[:, lanes] = total[row : row + slab]
    for peer in range(copies.shape[0]):
        copies[peer] = image[...]
    sums[...] = total[len(where) * slab :]


def second_landing(*refs):
    *arrived, sums, first_image, scaling, own, correction, image = refs
    coefs = coefficients(sums)
    correction[...] = corrected(coefs, own[...], scaling[...], first_image[...])
    image[...] = summed(arrived, ...)


def small_call(body, out_shapes, args, scratch=(), spaces=None):
    spaces = spaces or [pltpu.VMEM] * len(out_shapes)
    return pl.pallas_call(
        body,
        in_specs=[pl.BlockSpec(memory_space=pltpu.VMEM)] * len(args),
        out_specs=[
            pl.BlockSpec() if space == pltpu.HBM else pl.BlockSpec(memory_space=space)
            for space in spaces
        ],
        out_shape=[
            pltpu.HBM(s, F32) if space == pltpu.HBM else jax.ShapeDtypeStruct(s, F32)
            for s, space in zip(out_shapes, spaces)
        ],
        scratch_shapes=scratch,
        compiler_params=pltpu.CompilerParams(vmem_limit_bytes=SMALL_VMEM),
    )(*args)


def per_device(wavefunction, precond, left_ops, right_ops, out_sector, live_counts):
    peers = lax.axis_size(TERM)
    width = wavefunction.shape[1]
    slab = width // peers
    split = (peers, slab, width)
    cuts = tuple(slab * share // sum(SHARES) for share in SHARES)
    size = lax.axis_size(TERM[0])
    field = wavefunction[0]
    blocked = field.reshape(split)
    scaling = precond[0]
    image_of = functools.partial(
        partial_image,
        counts=live_counts,
        targets=out_sector,
        left_stack=left_ops[0],
        right_stack=right_ops[0],
        split=split,
    )

    crossing, kept, local = image_of(first_kernel, fields=(field,), cuts=(slab,))
    crossed, local = moved(crossing, local)
    scaling_late, _ = lax.optimization_barrier((scaling, kept))
    full_scaling = swapped(jnp.broadcast_to(scaling_late[None], split))
    (packed,) = small_call(
        combine,
        [(peers, slab * (width // LANES) + EXTRA, LANES)],
        [kept, crossed, local, blocked, full_scaling],
        [pltpu.VMEM((EXTRA, LANES), F32)],
    )
    first_image, copies, sums = small_call(
        first_landing,
        [(slab, width), split, (EXTRA, LANES)],
        [swapped(packed)],
        spaces=[pltpu.VMEM, pltpu.HBM, pltpu.VMEM],
    )
    full_image = swapped(copies)
    sums = over_sectors(sums)

    fields = (sums, blocked, full_scaling, full_image)
    parts = image_of(second_kernel, fields=fields, cuts=cuts)
    crossing, kept, local = (parts[i * len(cuts) : (i + 1) * len(cuts)] for i in range(3))
    moves = [moved(c, l) for c, l in zip(crossing, local)]
    arrived = []
    for part, rows in enumerate(cuts):
        pieces = small_call(
            spread, [(size * rows, width)] * size, [kept[part], *moves[part]]
        )
        arrived += exchanged_along(pieces, TERM[0])
    pieces = small_call(relay, [(slab, width)] * size, arrived)
    arrived = exchanged_along(pieces, TERM[1])
    own = lax.dynamic_index_in_dim(blocked, lax.axis_index(TERM), 0, keepdims=False)
    correction, second_image = small_call(
        second_landing,
        [(slab, width)] * 2,
        [*arrived, sums, first_image, scaling, own],
    )
    return (first_image[None], correction[None], second_image[None])


def solution(mesh):
    torus = Mesh(mesh.devices.reshape(4, 4, 8, 2), ("term_0", "term_1", "sector_0", "sector_1"))
    placed = (
        P(SECTOR, None, None),
        P(SECTOR, TERM, None),
        P(SECTOR, TERM, None, None),
        P(SECTOR, TERM, None, None),
        P(SECTOR, TERM),
        P(SECTOR, TERM),
    )
    return jax.shard_map(
        per_device,
        mesh=torus,
        in_specs=placed,
        out_specs=(P(SECTOR, TERM, None), P(SECTOR, TERM, None), P(SECTOR, TERM, None)),
        check_vma=False,
    )
```

```python
import functools

import jax
import jax.numpy as jnp
from jax import lax
from jax.experimental import pallas as pl
from jax.experimental.pallas import tpu as pltpu
from jax.sharding import Mesh
from jax.sharding import PartitionSpec as P

TERM = ("term_0", "term_1")
SECTOR = ("sector_0", "sector_1")
LANES = 128
EXTRA = 8
HALVES = 2
MIB = 1 << 20
KERNEL_VMEM = 22 * MIB
SMALL_VMEM = 8 * MIB
F32 = jnp.float32


def moved(crossing, local):
    count = lax.axis_size(SECTOR)
    upward = [(i, i + 1) for i in range(1, count - 1, 2)]
    downward = [(j, i) for i, j in upward]
    swap = [(i, i ^ 1) for i in range(count)]
    return lax.ppermute(crossing, SECTOR, upward + downward), lax.ppermute(local, SECTOR, swap)


def exchanged_along(pieces, axis):
    size = len(pieces)
    routes = [[(i, (i + k) % size) for i in range(size)] for k in range(size)]
    farthest_first = sorted(range(1, size), key=lambda k: -min(k, size - k))
    sent = [lax.ppermute(pieces[k], axis, routes[k]) for k in farthest_first]
    return [*sent, pieces[0]]


def swapped(x):
    return lax.all_to_all(x, TERM, 0, 0, tiled=True)


def sector_steps():
    for axis in SECTOR[::-1]:
        count = lax.axis_size(axis)
        mask = 1
        while mask < count:
            yield functools.partial(exchanged, axis=axis, mask=mask)
            mask *= 2


def exchanged(x, axis, mask):
    pairs = [(i, i ^ mask) for i in range(lax.axis_size(axis))]
    return x + lax.ppermute(x, axis, pairs)


def over_sectors(x):
    for step in sector_steps():
        x = step(x)
    return x


def halves(x):
    high = x.astype(jnp.bfloat16)
    low = (x - high.astype(F32)).astype(jnp.bfloat16)
    return high, low


def product(a_high, a_low, b_high, b_low):
    dot = functools.partial(jnp.dot, preferred_element_type=F32)
    return dot(a_high, b_high) + (dot(a_high, b_low) + dot(a_low, b_high))


def fetches(slot, stacks, held, landed):
    return [
        pltpu.make_async_copy(stack.at[slot], place.at[slot], landed.at[i, slot])
        for i, (stack, place) in enumerate(zip(stacks, held))
    ]


def begin(stacks, held, landed, outs):
    for fetch in fetches(0, stacks, held, landed):
        fetch.start()
    for out in outs:
        out[...] = jnp.zeros_like(out)


def accumulate(sector, count, target, stacks, held, landed, field_high, field_low, outs):
    slot = pl.program_id(0)
    peers, rows, width = outs[0].shape

    @pl.when(slot < count[0, 0])
    def _():
        for fetch in fetches(slot, stacks, held, landed):
            fetch.wait()
        for later in range(1, stacks[0].shape[0]):

            @pl.when((slot == 0) & (later < count[0, 0]))
            def _(later=later):
                for fetch in fetches(later, stacks, held, landed):
                    fetch.start()

        left, right = held
        left_high, left_low = halves(left[slot])
        inner = product(left_high, left_low, field_high[...], field_low[...])
        inner_high, inner_low = halves(inner)
        right_high, right_low = halves(right[slot])
        result = product(inner_high, inner_low, right_high, right_low)
        goal = target[0, slot]
        kept = goal == sector
        swapped_here = goal == (sector ^ 1)
        roles = (jnp.logical_not(kept | swapped_here), kept, swapped_here)
        cuts = len(outs) // len(roles)
        result = result.reshape(peers, cuts * rows, width)
        for i, role in enumerate(roles):

            @pl.when(role)
            def _(i=i):
                for cut in range(cuts):
                    outs[i * cuts + cut][...] += result[:, cut * rows : (cut + 1) * rows]


def first_kernel(count, target, left, right, field, *rest):
    *outs, f_high, f_low, held_left, held_right, landed, whole, arrived = rest
    stacks, held = (left, right), (held_left, held_right)

    @pl.when(pl.program_id(0) == 0)
    def _():
        fetch = pltpu.make_async_copy(field, whole, arrived)
        fetch.start()
        begin(stacks, held, landed, outs)
        fetch.wait()
        f_high[...], f_low[...] = halves(whole[...])

    sector = lax.axis_index(SECTOR)
    accumulate(sector, count, target, stacks, held, landed, f_high, f_low, outs)


def coefficients(sums):
    cross, norm_sq = sums[0:1, 0:1], sums[1:2, 0:1]
    scaled_cross, scaled_norm = sums[2:3, 0:1], sums[3:4, 0:1]
    rayleigh = cross / norm_sq
    return rayleigh, (scaled_cross - rayleigh * scaled_norm) / norm_sq


def corrected(coefs, vector, scaling, image):
    rayleigh, share = coefs
    return scaling * (image - rayleigh * vector) - share * vector


def second_kernel(count, target, left, right, sums, field, scaling, image, *rest):
    *outs, f_high, f_low, held_left, held_right, landed = rest
    stacks, held = (left, right), (held_left, held_right)
    peers, slab, width = field.shape

    @pl.when(pl.program_id(0) == 0)
    def _():
        begin(stacks, held, landed, outs)
        coefs = coefficients(sums)
        for peer in range(peers):
            value = corrected(coefs, field[peer], scaling[peer], image[peer])
            f_high[peer], f_low[peer] = halves(value)

    flat = (peers * slab, width)
    f_high, f_low = f_high.reshape(flat), f_low.reshape(flat)
    sector = lax.axis_index(SECTOR)
    accumulate(sector, count, target, stacks, held, landed, f_high, f_low, outs)


def partial_image(body, counts, targets, left_stack, right_stack, fields, cuts, split):
    slots, width, _ = right_stack.shape
    in_vmem = pl.BlockSpec(memory_space=pltpu.VMEM)
    in_hbm = pl.BlockSpec(memory_space=pltpu.HBM)
    streamed = body is first_kernel
    targets, left_stack, right_stack = (
        pltpu.with_memory_space_constraint(x, pltpu.HBM)
        for x in (targets, left_stack, right_stack)
    )
    block = (width, width)
    part = (split[0], split[1] // cuts, width)
    scratch = [
        *[pltpu.VMEM(block if streamed else split, jnp.bfloat16)] * 2,
        *[pltpu.VMEM((slots, *block), F32)] * 2,
        pltpu.SemaphoreType.DMA((2, slots)),
    ]
    if streamed:
        fields = [pltpu.with_memory_space_constraint(x, pltpu.HBM) for x in fields]
        scratch += [pltpu.VMEM(block, F32), pltpu.SemaphoreType.DMA]
    return pl.pallas_call(
        body,
        out_shape=[jax.ShapeDtypeStruct(part, F32)] * (3 * cuts),
        grid_spec=pltpu.PrefetchScalarGridSpec(
            num_scalar_prefetch=1,
            grid=(slots,),
            in_specs=[
                pl.BlockSpec(targets.shape, lambda i, *_: (0, 0), memory_space=pltpu.SMEM),
                in_hbm,
                in_hbm,
                *[in_hbm if streamed else in_vmem] * len(fields),
            ],
            out_specs=[in_vmem] * (3 * cuts),
            scratch_shapes=scratch,
        ),
        compiler_params=pltpu.CompilerParams(
            dimension_semantics=("arbitrary",), vmem_limit_bytes=KERNEL_VMEM
        ),
        cost_estimate=pl.CostEstimate(
            flops=slots * 12 * width**3, bytes_accessed=slots * 8 * width**2, transcendentals=0
        ),
    )(counts, targets, left_stack, right_stack, *fields)


def place(half, along, across, size):
    return along * size + across if half == 0 else across * size + along


def spread(half, kept, crossed, local, *pieces):
    rows = kept.shape[1]
    size = len(pieces)
    me = lax.axis_index(TERM[half])
    for k, piece in enumerate(pieces):
        for across in range(size):
            peer = place(half, lax.rem(me + k, size), across, size)
            total = kept[peer] + (crossed[peer] + local[peer])
            piece[across * rows : (across + 1) * rows] = total


def relay(axis, rows, *refs):
    size = len(refs) // 2
    arrived, pieces = refs[:size], refs[size:]
    me = lax.axis_index(axis)
    for k, piece in enumerate(pieces):
        lines = pl.ds(pl.multiple_of(lax.rem(me + k, size) * rows, rows), rows)
        piece[...] = functools.reduce(lambda x, y: x + y, [ref[lines] for ref in arrived])


def landed(refs):
    size = len(refs) // HALVES
    groups = [refs[h * size : (h + 1) * size] for h in range(HALVES)]
    return [functools.reduce(lambda x, y: x + y, [r[...] for r in g]) for g in groups]


def tiles(x, slab, width):
    return [(c * slab, slice(c * LANES, (c + 1) * LANES)) for c in range(width // LANES)]


def combine(kept, crossed, local, field, scaling, packed, tail):
    peers, slab, width = kept.shape
    where = tiles(kept, slab, width)
    cross = scaled_cross = jnp.zeros((slab, width), F32)
    for peer in range(peers):
        total = kept[peer] + (crossed[peer] + local[peer])
        for row, lanes in where:
            packed[peer, row : row + slab] = total[:, lanes]
        weighted = field[peer] * total
        cross += weighted
        scaled_cross += scaling[peer] * weighted
    me = lax.axis_index(TERM)
    own = field[me]
    square = own * own
    line = lax.broadcasted_iota(jnp.int32, tail.shape, 0)
    tile = jnp.zeros(tail.shape, F32)
    for i, part in enumerate((cross, square, scaled_cross, scaling[me] * square)):
        tile = jnp.where(line == i, jnp.sum(part, keepdims=True), tile)
    tail[...] = tile
    for peer in range(peers):
        packed[peer, len(where) * slab :] = tail[...]


def first_landing(arrived, image, copies, sums):
    slab, width = image.shape
    total = functools.reduce(lambda x, y: x + y, [arrived[i] for i in range(arrived.shape[0])])
    where = tiles(image, slab, width)
    for row, lanes in where:
        image[:, lanes] = total[row : row + slab]
    for peer in range(copies.shape[0]):
        copies[peer] = image[...]
    sums[...] = total[len(where) * slab :]


def second_landing(*refs):
    *arrived, sums, first_image, scaling, own, correction, image = refs
    rows = image.shape[0] // HALVES
    coefs = coefficients(sums)
    correction[...] = corrected(coefs, own[...], scaling[...], first_image[...])
    for half, total in enumerate(landed(arrived)):
        image[half * rows : (half + 1) * rows] = total


def relayed(half, pieces, rows):
    arrived = exchanged_along(pieces, TERM[half])
    other = TERM[1 - half]
    shape = (rows, pieces[0].shape[1])
    onward = small_call(
        functools.partial(relay, other, rows), [shape] * len(pieces), arrived
    )
    return exchanged_along(onward, other)


def small_call(body, out_shapes, args, scratch=(), spaces=None):
    spaces = spaces or [pltpu.VMEM] * len(out_shapes)
    return pl.pallas_call(
        body,
        in_specs=[pl.BlockSpec(memory_space=pltpu.VMEM)] * len(args),
        out_specs=[
            pl.BlockSpec() if space == pltpu.HBM else pl.BlockSpec(memory_space=space)
            for space in spaces
        ],
        out_shape=[
            pltpu.HBM(s, F32) if space == pltpu.HBM else jax.ShapeDtypeStruct(s, F32)
            for s, space in zip(out_shapes, spaces)
        ],
        scratch_shapes=scratch,
        compiler_params=pltpu.CompilerParams(vmem_limit_bytes=SMALL_VMEM),
    )(*args)


def per_device(wavefunction, precond, left_ops, right_ops, out_sector, live_counts):
    peers = lax.axis_size(TERM)
    width = wavefunction.shape[1]
    slab = width // peers
    split = (peers, slab, width)
    rows = slab // HALVES
    size = lax.axis_size(TERM[0])
    field = wavefunction[0]
    blocked = field.reshape(split)
    scaling = precond[0]
    image_of = functools.partial(
        partial_image,
        counts=live_counts,
        targets=out_sector,
        left_stack=left_ops[0],
        right_stack=right_ops[0],
        split=split,
    )

    crossing, kept, local = image_of(first_kernel, fields=(field,), cuts=1)
    crossed, local = moved(crossing, local)
    scaling_late, _ = lax.optimization_barrier((scaling, kept))
    full_scaling = swapped(jnp.broadcast_to(scaling_late[None], split))
    (packed,) = small_call(
        combine,
        [(peers, slab * (width // LANES) + EXTRA, LANES)],
        [kept, crossed, local, blocked, full_scaling],
        [pltpu.VMEM((EXTRA, LANES), F32)],
    )
    first_image, copies, sums = small_call(
        first_landing,
        [(slab, width), split, (EXTRA, LANES)],
        [swapped(packed)],
        spaces=[pltpu.VMEM, pltpu.HBM, pltpu.VMEM],
    )
    full_image = swapped(copies)
    sums = over_sectors(sums)

    fields = (sums, blocked, full_scaling, full_image)
    parts = image_of(second_kernel, fields=fields, cuts=HALVES)
    crossing, kept, local = (parts[i * HALVES : (i + 1) * HALVES] for i in range(3))
    moves = [moved(c, l) for c, l in zip(crossing, local)]
    arrived = []
    for half in range(HALVES):
        pieces = small_call(
            functools.partial(spread, half),
            [(size * rows, width)] * size,
            [kept[half], *moves[half]],
        )
        arrived += relayed(half, pieces, rows)
    own = lax.dynamic_index_in_dim(blocked, lax.axis_index(TERM), 0, keepdims=False)
    correction, second_image = small_call(
        second_landing,
        [(slab, width)] * 2,
        [*arrived, sums, first_image, scaling, own],
    )
    return (first_image[None], correction[None], second_image[None])


def solution(mesh):
    torus = Mesh(mesh.devices.reshape(4, 4, 8, 2), ("term_0", "term_1", "sector_0", "sector_1"))
    placed = (
        P(SECTOR, None, None),
        P(SECTOR, TERM, None),
        P(SECTOR, TERM, None, None),
        P(SECTOR, TERM, None, None),
        P(SECTOR, TERM),
        P(SECTOR, TERM),
    )
    return jax.shard_map(
        per_device,
        mesh=torus,
        in_specs=placed,
        out_specs=(P(SECTOR, TERM, None), P(SECTOR, TERM, None), P(SECTOR, TERM, None)),
        check_vma=False,
    )
```
